32 devices in a mesh: ens: 2 (over y), lon: 4 (over z), lat: 2 (over x), ch: 2 (over core).
Axes of the slice: x: 2, y: 2, z: 4, core: 2. Of those that a mesh axis runs over, the one named last changes fastest.
Arguments:
- input_field: bfloat16 [256, 128, 128], P(('ens', 'lat', 'ch'), 'lon'), parts along dimension 0, may hold values from -6 to 6
- encoder_filter: bfloat16 [128, 4, 5], P(('lat', 'ch')), may hold values from -2.6875 to 2.6875
- row_owner: int32 [256], P(('ens', 'lat', 'ch')), parts along dimension 0, may hold values from 0 to 63, as said below
- encoder_weight: bfloat16 [512, 256], replicated, may hold values from -0.25 to 0.25
- disco_basis: bfloat16 [64, 4, 3, 17], P(('lat', 'ch')), may hold values from -1.5 to 1.5
- row_widths: int32 [64], P(('lat', 'ch')), may hold values from 1 to 8, as said below
- block_weights: bfloat16 [2, 1024, 256], replicated, may hold values from -0.1875 to 0.1875
- cotangent: bfloat16 [128, 64, 256], P(('ens', 'lat', 'ch'), 'lon'), parts along dimension 0, may hold values from -6 to 6
Outputs:
- state_out: bfloat16 [128, 64, 256], P(('ens', 'lat', 'ch'), 'lon'), parts along dimension 0
- latent_grad: bfloat16 [128, 64, 256], P(('ens', 'lat', 'ch'), 'lon'), parts along dimension 0
- block_grads: float32 [4, 1024, 256], P('ens', None, 'ch'), parts along dimension 0
- encoder_grad: float32 [1024, 256], P('ens', 'ch'), parts along dimension 0
The draws below stay inside these ranges and needn't reach their ends.
There are 2 independent parts, one for each index of `ens`. The reference program is written for one: setup_inputs(seed, part) draws one part's arguments, and reference() takes and returns one part's arrays. A program takes and returns all parts, laid end to end along the dimension named above; an argument that names none is the same for every part. Nothing has to cross between parts.
Inputs may be any that keep to these rules, and one draw needn't show every extreme that they name: `row_owner`: input row p feeds latent row (p - 1) // 2, p // 2 or (p + 1) // 2, and every latent row is fed by 1 to 3 input rows. `row_widths`: the first and last rows have 8.
All inputs are finite; a program needn't handle non-finite values.
Results may differ from the reference program's by a relative error of at most 0.014.
Values may be sent and summed in bfloat16 or wider, within the bound.
A program may use at most 64 MiB of HBM per device.

```python
import math
import jax
import jax.numpy as jnp
from jax import lax

CHANNELS = 256
IN_CHANNELS = 128
BASIS = 4
REACH = 8
TAP_REACH = 2
BLOCKS = 2
ROWS_DEV = 16
NLAT = 64
NLON = 64
NLAT_IN = 128
NLON_IN = 128


def draw_row_owner(key, part):
    key_moves = jax.random.fold_in(key, 11)
    position = jnp.arange(NLAT + 1, dtype=jnp.int32)
    stepping = jax.random.randint(key_moves, (NLAT + 1,), -1, 2, dtype=jnp.int32)
    drifts = jnp.where(position % 2 == 1, 0, stepping)
    at_edge = position % ROWS_DEV == 0
    drifts = jnp.where(at_edge, 0, drifts)
    starts = 2 * position + drifts
    input_rows = jnp.arange(2 * NLAT, dtype=jnp.int32)
    inside = (starts[None, 1:NLAT] <= input_rows[:, None]).astype(jnp.int32)
    owners = jnp.sum(inside, axis=1).astype(jnp.int32)
    band_rows = 2 * ROWS_DEV
    first_of_band = (input_rows % band_rows == 0) & (input_rows > 0)
    last_of_band = (input_rows % band_rows == band_rows - 1) & (input_rows < 2 * NLAT - 1)
    owners = jnp.where(first_of_band, owners - 1, owners)
    owners = jnp.where(last_of_band, owners + 1, owners)
    return owners.astype(jnp.int32)


def draw_row_widths(key, part):
    position = jnp.arange(NLAT, dtype=jnp.int32)
    distance = jnp.abs(2 * position + 1 - NLAT)
    jitter = jax.random.randint(jax.random.fold_in(key, 23), (NLAT,), 0, 2, dtype=jnp.int32)
    widths = 1 + jitter + (REACH - 2) * distance * distance // (NLAT * NLAT)
    widths = jnp.where((position == 0) | (position == NLAT - 1), REACH, widths)
    return jnp.clip(widths, 1, REACH).astype(jnp.int32)


def block_levels(own_key, extent, cuts, smallest, top_value):
    factor_of, own = 1.0, jax.random.fold_in(own_key, 6)
    for dim, shards_of in cuts:
        draws = jnp.exp(jax.random.uniform(jax.random.fold_in(own, dim), (shards_of,), jnp.float32, smallest / len(cuts), top_value / len(cuts)))
        factor_of = factor_of * jnp.repeat(draws, extent[dim] // shards_of).reshape([-1 if axis == dim else 1 for axis in range(len(extent))])
    return factor_of


def bell_draw(rng, dims, width, limit, shards=(), held_as=jnp.bfloat16):
    entries = width * jax.random.normal(rng, dims, jnp.float32)
    if shards:
        entries = entries * block_levels(rng, dims, shards, -0.22, 0.18)
    return jnp.clip(entries, -limit, limit).astype(held_as)


def setup_inputs(seed: int = 0, part: int = 0) -> dict:
    splits = jax.random.split(jax.random.key(seed), 9)
    part_keys = jax.random.split(jax.random.fold_in(splits[8], part), 9)
    return {
        "input_field": bell_draw(part_keys[0], (NLAT_IN, NLON_IN, IN_CHANNELS), 1.0, 6.0, ((0, 4), (1, 4))),
        "encoder_filter": bell_draw(splits[1], (NLAT_IN, BASIS, 2 * TAP_REACH + 1), 0.45, 2.6875, ((0, 4),)),
        "row_owner": draw_row_owner(jax.random.fold_in(jax.random.fold_in(splits[8], part), 71), part),
        "encoder_weight": bell_draw(splits[3], (BASIS * IN_CHANNELS, CHANNELS), (BASIS * IN_CHANNELS) ** -0.5, 0.25),
        "disco_basis": bell_draw(splits[4], (NLAT, BASIS, 3, 2 * REACH + 1), 0.25, 1.5, ((0, 4),)),
        "row_widths": draw_row_widths(jax.random.fold_in(splits[8], 71), part),
        "block_weights": bell_draw(splits[6], (BLOCKS, BASIS * CHANNELS, CHANNELS), (BASIS * CHANNELS) ** -0.5, 0.1875),
        "cotangent": bell_draw(part_keys[7], (NLAT, NLON, CHANNELS), 1.0, 6.0, ((0, 4), (1, 4))),
    }


def masked_basis(disco_basis, row_widths):
    offsets = jnp.abs(jnp.arange(2 * REACH + 1, dtype=jnp.int32) - REACH)
    keep = offsets[None, :] <= row_widths[:, None]
    values = disco_basis.astype(jnp.float32)
    return jnp.where(keep[:, None, None, :], values, jnp.zeros_like(values))

def apply_stencil(field, basis):
    padded = jnp.pad(field, ((1, 1), (0, 0), (0, 0)))
    padded = jnp.concatenate([padded[:, NLON - REACH:], padded, padded[:, :REACH]], axis=1)
    stacked = jnp.stack([padded[0:NLAT], padded[1:NLAT + 1], padded[2:NLAT + 2]], axis=0)
    result = jnp.zeros((NLAT, NLON, BASIS, CHANNELS), field.dtype)
    for shift_col in range(2 * REACH + 1):
        window = stacked[:, :, shift_col:shift_col + NLON, :]
        result = result + jnp.einsum('rijc,ikr->ijkc', window, basis[:, :, :, shift_col], precision=lax.Precision.HIGHEST)
    return result

def reference(input_field, encoder_filter, row_owner, encoder_weight, disco_basis, row_widths, block_weights, cotangent):
    field_in = input_field.astype(jnp.float32)
    wrapped = jnp.concatenate([field_in[:, NLON_IN - TAP_REACH:], field_in, field_in[:, :TAP_REACH]], axis=1)
    filter_values = encoder_filter.astype(jnp.float32)
    accumulated = jnp.zeros((NLAT_IN, NLON, BASIS, IN_CHANNELS), field_in.dtype)
    for tap_index in range(2 * TAP_REACH + 1):
        sampled = wrapped[:, tap_index:tap_index + NLON_IN:2, :]
        accumulated = accumulated + sampled[:, :, None, :] * filter_values[:, None, :, tap_index, None]
    filtered_input = accumulated.astype(jnp.bfloat16)
    regridded = jax.ops.segment_sum(filtered_input.astype(jnp.float32), row_owner, num_segments=NLAT)
    latent_input = regridded.astype(jnp.bfloat16).reshape(NLAT * NLON, BASIS * IN_CHANNELS)
    current = jnp.dot(latent_input, encoder_weight, preferred_element_type=jnp.float32).astype(jnp.bfloat16)
    current = current.reshape(NLAT, NLON, CHANNELS)
    basis = masked_basis(disco_basis, row_widths)
    saved = []
    for layer_index in range(BLOCKS):
        features = apply_stencil(current.astype(jnp.float32), basis).astype(jnp.bfloat16)
        features = features.reshape(NLAT * NLON, BASIS * CHANNELS)
        preact = jnp.dot(features, block_weights[layer_index], preferred_element_type=jnp.float32)
        current = (current.astype(jnp.float32) + jax.nn.silu(preact).reshape(NLAT, NLON, CHANNELS)).astype(jnp.bfloat16)
        saved.append((features, preact))
    state_out = current
    zero_field = jnp.zeros((NLAT, NLON, CHANNELS), jnp.float32)
    unused, pullback = jax.vjp(lambda field: apply_stencil(field, basis), zero_field)
    gradient = cotangent
    weight_terms = [None] * BLOCKS
    for layer_index in reversed(range(BLOCKS)):
        features, preact = saved[layer_index]
        sigma = jax.nn.sigmoid(preact)
        upstream = gradient.reshape(NLAT * NLON, CHANNELS).astype(jnp.float32)
        act_grad = (upstream * sigma * (1.0 + preact * (1.0 - sigma))).astype(jnp.bfloat16)
        weight_terms[layer_index] = jnp.dot(features.T, act_grad, preferred_element_type=jnp.float32)
        errors = jnp.dot(act_grad, block_weights[layer_index].T, preferred_element_type=jnp.float32).astype(jnp.bfloat16)
        errors = errors.reshape(NLAT, NLON, BASIS, CHANNELS)
        spread = pullback(errors.astype(jnp.float32))[0]
        gradient = (gradient.astype(jnp.float32) + spread).astype(jnp.bfloat16)
    normalizer = 1.0 / math.sqrt(NLAT * NLON)
    encoder_term = jnp.dot(latent_input.T, gradient.reshape(NLAT * NLON, CHANNELS), preferred_element_type=jnp.float32)
    block_grads = jnp.stack(weight_terms, axis=0) * normalizer
    return (state_out, gradient, block_grads, encoder_term * normalizer)
```

```python
import functools
import math

import jax
import jax.numpy as jnp
from jax import lax
from jax.experimental import pallas as pl
from jax.experimental.pallas import tpu as pltpu
from jax.sharding import PartitionSpec as P

REACH = 8
TAP_REACH = 2
MESH = pl.DeviceIdType.MESH


class GradSum:
    def __init__(self, sizes, source, result, bufs, sems):
        self.lon, self.lat = sizes
        self.source, self.result = source, result
        self.rec_ch, self.part, self.rec_lon, self.piece, self.rec_lat, self.whole = bufs
        self.ssem, self.rsem = sems
        self.rows = part_rows = self.part.shape[0]
        self.span = part_rows // self.lon
        self.width = self.part.shape[1]
        self.my_lon = lax.axis_index("lon")
        self.my_lat = lax.axis_index("lat")
        self.my_ch = lax.axis_index("ch")
        self.pending = []

    @staticmethod
    def scratch(sizes, rows, width):
        lon, lat = sizes
        span = rows // lon
        count = 1 + 2 * (lon - 1) + (lat - 1)
        return [
            pltpu.VMEM((rows, width), jnp.bfloat16),
            pltpu.VMEM((rows, width), jnp.bfloat16),
            pltpu.VMEM((lon - 1, span, width), jnp.bfloat16),
            pltpu.VMEM((span, width), jnp.bfloat16),
            pltpu.VMEM((lat - 1, span, width), jnp.bfloat16),
            pltpu.VMEM((span, width), jnp.bfloat16),
            pltpu.SemaphoreType.DMA((count,)),
            pltpu.SemaphoreType.DMA((count,)),
        ]

    def send(self, source, target, slot, device):
        copy = pltpu.make_async_remote_copy(
            src_ref=source,
            dst_ref=target,
            send_sem=self.ssem.at[slot],
            recv_sem=self.rsem.at[slot],
            device_id=device,
            device_id_type=MESH,
        )
        copy.start()
        self.pending.append(copy)

    def settle(self):
        for copy in self.pending:
            copy.wait()
        self.pending = []

    def columns(self, half):
        return pl.ds(pl.multiple_of(half * self.width, self.width), self.width)

    def stretch(self, owner):
        return pl.ds(pl.multiple_of(owner * self.span, self.span), self.span)

    def start_ch(self):
        other = 1 - self.my_ch
        self.send(self.source.at[:, self.columns(other)], self.rec_ch, 0, {"ch": other})

    def start_lon(self):
        self.settle()
        own = self.source[:, self.columns(self.my_ch)].astype(jnp.float32)
        self.part[...] = (own + self.rec_ch[...].astype(jnp.float32)).astype(jnp.bfloat16)
        for step in range(1, self.lon):
            peer = lax.rem(self.my_lon + step, self.lon)
            self.send(
                self.part.at[self.stretch(peer)], self.rec_lon.at[step - 1], step, {"lon": peer}
            )

    def start_lat(self):
        self.settle()
        total = self.part[self.stretch(self.my_lon), :].astype(jnp.float32)
        for step in range(1, self.lon):
            total = total + self.rec_lon[step - 1].astype(jnp.float32)
        self.piece[...] = total.astype(jnp.bfloat16)
        for step in range(1, self.lat):
            peer = lax.rem(self.my_lat + step, self.lat)
            self.send(self.piece, self.rec_lat.at[step - 1], self.lon + step - 1, {"lat": peer})

    def start_gather(self):
        self.settle()
        total = self.piece[...].astype(jnp.float32)
        for step in range(1, self.lat):
            total = total + self.rec_lat[step - 1].astype(jnp.float32)
        self.whole[...] = total.astype(jnp.bfloat16)
        own = self.stretch(self.my_lon)
        self.result[own, :] = self.whole[...]
        for step in range(1, self.lon):
            peer = lax.rem(self.my_lon + step, self.lon)
            slot = self.lon + self.lat - 2 + step
            self.send(self.whole, self.result.at[own], slot, {"lon": peer})

    def finish(self):
        self.settle()


def greet(sizes):
    lon, lat = sizes
    barrier = pltpu.get_barrier_semaphore()
    my_lon, my_lat, my_ch = (lax.axis_index(name) for name in ("lon", "lat", "ch"))
    pl.semaphore_signal(barrier, inc=1, device_id={"ch": 1 - my_ch}, device_id_type=MESH)
    for step in range(1, lon):
        peer = lax.rem(my_lon + step, lon)
        pl.semaphore_signal(barrier, inc=1, device_id={"lon": peer}, device_id_type=MESH)
    for step in range(1, lat):
        peer = lax.rem(my_lat + step, lat)
        pl.semaphore_signal(barrier, inc=1, device_id={"lat": peer}, device_id_type=MESH)
    pl.semaphore_wait(barrier, lon + lat - 1)


def sum_kernel(sizes, count, *refs):
    sources, results, rest = refs[:count], refs[count : 2 * count], refs[2 * count :]
    greet(sizes)
    sums = []
    for index in range(count):
        mine = rest[8 * index : 8 * index + 8]
        sums.append(GradSum(sizes, sources[index], results[index], mine[:6], mine[6:]))
    stages = ("start_ch", "start_lon", "start_lat", "start_gather", "finish")
    for tick in range(count + len(stages) - 1):
        for index in range(count):
            if 0 <= tick - index < len(stages):
                getattr(sums[index], stages[tick - index])()


def summed_grads(terms, sizes):
    width = terms[0].shape[1] // 2
    scratch = []
    for term in terms:
        scratch += GradSum.scratch(sizes, term.shape[0], width)
    vmem = pl.BlockSpec(memory_space=pltpu.VMEM)
    return pl.pallas_call(
        functools.partial(sum_kernel, sizes, len(terms)),
        out_shape=[jax.ShapeDtypeStruct((t.shape[0], width), jnp.bfloat16) for t in terms],
        in_specs=[vmem] * len(terms),
        out_specs=[vmem] * len(terms),
        scratch_shapes=scratch,
        compiler_params=pltpu.CompilerParams(
            collective_id=0, has_side_effects=True, vmem_limit_bytes=48 << 20
        ),
    )(*terms)


def passed_along(value, axis, steps):
    count = lax.axis_size(axis)
    pairs = [(source, (source + steps) % count) for source in range(count)]
    return lax.ppermute(value, axis, pairs)


def from_behind(block, axis, distance):
    devices = range(lax.axis_size(axis))
    route = [(i - distance, i) for i in devices if i - distance in devices]
    return lax.ppermute(block, axis, route)


def padded(block, sides, width, periodic):
    for axis, dim in sides:
        count = lax.axis_size(axis)
        forward = [(i, i + 1) for i in range(count - 1)]
        if periodic:
            forward.append((count - 1, 0))
        backward = [(target, source) for source, target in forward]
        low = lax.ppermute(
            lax.slice_in_dim(block, block.shape[dim] - width, None, axis=dim), axis, forward
        )
        high = lax.ppermute(lax.slice_in_dim(block, 0, width, axis=dim), axis, backward)
        block = jnp.concatenate([low, block, high], axis=dim)
    return block


def add_edges(middle, to_first, to_last):
    row_count = middle.shape[0]
    rest_pads = [(0, 0)] * (middle.ndim - 1)
    lower = jnp.pad(to_first, [(0, row_count - 1)] + rest_pads)
    upper = jnp.pad(to_last, [(row_count - 1, 0)] + rest_pads)
    return middle + lower + upper


def apply_basis(banded, extended, rows_dev):
    accumulated = None
    for shift_row in range(3):
        term = jnp.einsum(
            "ikjq,iqc->ijkc",
            banded[:, :, shift_row],
            extended[shift_row : shift_row + rows_dev],
            preferred_element_type=jnp.float32,
        )
        accumulated = term if accumulated is None else accumulated + term
    return accumulated


def spread_basis(banded, errors):
    pieces = [
        jnp.einsum(
            "ikjq,ijkc->iqc", banded[:, :, shift_row], errors, preferred_element_type=jnp.float32
        )
        for shift_row in range(3)
    ]
    first = jnp.pad(pieces[0], ((0, 2), (0, 0), (0, 0)))
    second = jnp.pad(pieces[1], ((1, 1), (0, 0), (0, 0)))
    third = jnp.pad(pieces[2], ((2, 0), (0, 0), (0, 0)))
    return first + second + third


def return_rims(spread, cols_dev):
    left_rim = spread[:, :REACH]
    right_rim = spread[:, REACH + cols_dev :]
    interior = spread[:, REACH : REACH + cols_dev]
    from_east = passed_along(left_rim.astype(jnp.bfloat16), "lon", -1).astype(left_rim.dtype)
    from_west = passed_along(right_rim.astype(jnp.bfloat16), "lon", 1).astype(right_rim.dtype)
    interior = interior + jnp.pad(from_west, ((0, 0), (0, cols_dev - REACH), (0, 0)))
    interior = interior + jnp.pad(from_east, ((0, 0), (cols_dev - REACH, 0), (0, 0)))
    row_total = interior.shape[0]
    from_above = from_behind(interior[0:1], ("lat", "ch"), -1)
    from_below = from_behind(interior[row_total - 1 :], ("lat", "ch"), 1)
    return add_edges(interior[1 : row_total - 1], from_below, from_above)


def per_device(
    input_field,
    encoder_filter,
    row_owner,
    encoder_weight,
    disco_basis,
    row_widths,
    block_weights,
    cotangent,
):
    rows_in, cols_in, in_width = input_field.shape
    rows_dev = rows_in // 2
    cols_dev = cols_in // 2
    basis_count = encoder_filter.shape[1]
    tap_count = encoder_filter.shape[2]
    channels = block_weights.shape[2]
    layers = block_weights.shape[0]
    cell_count = rows_dev * cols_dev
    extended_in = padded(input_field, (("lon", 1),), TAP_REACH, True)
    filter_values = encoder_filter.astype(jnp.float32)
    accumulated = jnp.zeros((rows_in, cols_dev, basis_count, in_width), jnp.float32)
    for tap_index in range(tap_count):
        sampled = extended_in[:, tap_index : tap_index + cols_in : 2, :]
        accumulated = (
            accumulated
            + sampled[:, :, None, :].astype(jnp.float32)
            * filter_values[:, None, :, tap_index, None]
        )
    filtered_in = accumulated.astype(jnp.bfloat16).reshape(
        rows_in, cols_dev * basis_count * in_width
    )
    first_row = lax.axis_index(("lat", "ch")) * rows_dev
    relative = row_owner - first_row + 1
    selector = (relative[None, :] == jnp.arange(rows_dev + 2, dtype=jnp.int32)[:, None]).astype(
        jnp.bfloat16
    )
    summed = jnp.dot(selector, filtered_in, preferred_element_type=jnp.float32)
    from_above = from_behind(summed[0:1].astype(jnp.bfloat16), ("lat", "ch"), -1).astype(
        jnp.float32
    )
    from_below = from_behind(summed[rows_dev + 1 :].astype(jnp.bfloat16), ("lat", "ch"), 1).astype(
        jnp.float32
    )
    regridded = add_edges(summed[1 : rows_dev + 1], from_below, from_above)
    latent_in = regridded.astype(jnp.bfloat16).reshape(cell_count, basis_count * in_width)
    current = jnp.dot(latent_in, encoder_weight, preferred_element_type=jnp.float32).astype(
        jnp.bfloat16
    )
    current = current.reshape(rows_dev, cols_dev, channels)
    offsets = jnp.abs(jnp.arange(2 * REACH + 1, dtype=jnp.int32) - REACH)
    keep = offsets[None, :] <= row_widths[:, None]
    masked = jnp.where(keep[:, None, None, :], disco_basis, jnp.zeros_like(disco_basis))
    ext_cols = cols_dev + 2 * REACH
    differences = (
        jnp.arange(ext_cols, dtype=jnp.int32)[None, :]
        - jnp.arange(cols_dev, dtype=jnp.int32)[:, None]
    )
    placement = (
        differences[:, :, None] == jnp.arange(2 * REACH + 1, dtype=jnp.int32)[None, None, :]
    ).astype(jnp.bfloat16)
    banded = jnp.einsum(
        "ikrt,jqt->ikrjq", masked, placement, preferred_element_type=jnp.float32
    ).astype(jnp.bfloat16)
    saved = []
    for layer_index in range(layers):
        rows_ext = padded(current, ((("lat", "ch"), 0),), 1, False)
        extended = padded(rows_ext, (("lon", 1),), REACH, True)
        features = (
            apply_basis(banded, extended, rows_dev)
            .astype(jnp.bfloat16)
            .reshape(cell_count, basis_count * channels)
        )
        preact = jnp.dot(features, block_weights[layer_index], preferred_element_type=jnp.float32)
        current = (
            current.astype(jnp.float32) + jax.nn.silu(preact).reshape(rows_dev, cols_dev, channels)
        ).astype(jnp.bfloat16)
        saved.append((features, preact))
    gradient = cotangent
    weight_terms = [None] * layers
    for layer_index in reversed(range(layers)):
        features, preact = saved[layer_index]
        sigma = jax.nn.sigmoid(preact)
        upstream = gradient.reshape(cell_count, channels).astype(jnp.float32)
        act_grad = (upstream * sigma * (1.0 + preact * (1.0 - sigma))).astype(jnp.bfloat16)
        weight_terms[layer_index] = lax.dot_general(
            features, act_grad, (((0,), (0,)), ((), ())), preferred_element_type=jnp.float32
        )
        errors = lax.dot_general(
            act_grad,
            block_weights[layer_index],
            (((1,), (1,)), ((), ())),
            preferred_element_type=jnp.float32,
        )
        errors = errors.astype(jnp.bfloat16).reshape(rows_dev, cols_dev, basis_count, channels)
        spread = spread_basis(banded, errors)
        returned = return_rims(spread, cols_dev)
        gradient = (gradient.astype(jnp.float32) + returned).astype(jnp.bfloat16)
    encoder_term = lax.dot_general(
        latent_in,
        gradient.reshape(cell_count, channels),
        (((0,), (0,)), ((), ())),
        preferred_element_type=jnp.float32,
    )
    own_width = channels // lax.axis_size("ch")
    sizes = (lax.axis_size("lon"), lax.axis_size("lat"))
    terms = [term.astype(jnp.bfloat16) for term in weight_terms[::-1] + [encoder_term]]
    sums = [value.astype(jnp.float32) for value in summed_grads(terms, sizes)]
    block_sum, encoder_sum = jnp.stack(sums[:-1][::-1]), sums[-1]
    cells_total = cell_count * lax.axis_size("lon") * lax.axis_size(("lat", "ch"))
    normalizer = 1.0 / math.sqrt(cells_total)
    block_grads = (block_sum * normalizer).reshape(layers, basis_count * channels, own_width)
    encoder_grad = encoder_sum * normalizer
    return (current, gradient, block_grads, encoder_grad)


def solution(mesh):
    placed = (
        P(("ens", "lat", "ch"), "lon", None),
        P(("lat", "ch"), None, None),
        P(("ens", "lat", "ch")),
        P(),
        P(("lat", "ch"), None, None, None),
        P(("lat", "ch")),
        P(),
        P(("ens", "lat", "ch"), "lon", None),
    )
    return jax.shard_map(
        per_device,
        mesh=mesh,
        in_specs=placed,
        out_specs=(
            P(("ens", "lat", "ch"), "lon", None),
            P(("ens", "lat", "ch"), "lon", None),
            P("ens", None, "ch"),
            P("ens", "ch"),
        ),
        check_vma=False,
    )
```

```python
import functools
import math

import jax
import jax.numpy as jnp
from jax import lax
from jax.experimental import pallas as pl
from jax.experimental.pallas import tpu as pltpu
from jax.sharding import PartitionSpec as P

REACH = 8
TAP_REACH = 2
TILE = 16
MESH = pl.DeviceIdType.MESH
BF16 = jnp.bfloat16
F32 = jnp.float32


def along(axis, steps):
    count = lax.axis_size(axis)
    return {axis: lax.rem(lax.axis_index(axis) + steps + count, count)}


def neighbour(row_step, col_step):
    ch_count = lax.axis_size("ch")
    bands = lax.axis_size("lat") * ch_count
    band = lax.axis_index("lat") * ch_count + lax.axis_index("ch")
    band = lax.rem(band + row_step + bands, bands)
    target = {}
    if row_step:
        target = {"lat": band // ch_count, "ch": lax.rem(band, ch_count)}
    if col_step:
        target.update(along("lon", col_step))
    return target


AROUND = [(r, c) for r in (-1, 0, 1) for c in (-1, 0, 1) if r or c]


def greet():
    targets = [neighbour(r, c) for r, c in AROUND]
    for axis in ("ch", "lat", "lon"):
        targets += [along(axis, step) for step in range(1, lax.axis_size(axis))]
    barrier = pltpu.get_barrier_semaphore()
    for target in targets:
        pl.semaphore_signal(barrier, inc=1, device_id=target, device_id_type=MESH)
    pl.semaphore_wait(barrier, len(targets))


class Sender:
    def __init__(self, sems):
        self.ssem, self.rsem = sems
        self.pending = []

    def send(self, source, target, slot, device):
        copy = pltpu.make_async_remote_copy(
            src_ref=source,
            dst_ref=target,
            send_sem=self.ssem.at[slot],
            recv_sem=self.rsem.at[slot],
            device_id=device,
            device_id_type=MESH,
        )
        copy.start()
        self.pending.append(copy)

    def settle(self):
        for copy in self.pending:
            copy.wait()
        self.pending = []


class GradSum(Sender):
    def __init__(self, result, bufs):
        super().__init__(bufs[-2:])
        self.result = result
        self.source, self.rec_ch, self.part, self.rec_lat, self.strip, self.rec_lon, self.piece = bufs[:-2]
        self.width = self.part.shape[1]
        self.lat, self.lon = lax.axis_size("lat"), lax.axis_size("lon")
        self.height = self.strip.shape[0]
        self.span = self.piece.shape[0]
        self.split = self.span < self.height

    @staticmethod
    def scratch(sizes, rows, columns):
        lat, lon = sizes
        width = columns // 2
        height = rows // lat
        span = height // lon if height % (lon * TILE) == 0 else height
        count = 1 + 2 * (lat - 1) + 2 * (lon - 1)
        return [
            pltpu.VMEM((rows, columns), BF16),
            pltpu.VMEM((rows, width), BF16),
            pltpu.VMEM((rows, width), BF16),
            pltpu.VMEM((lat - 1, height, width), BF16),
            pltpu.VMEM((height, width), BF16),
            pltpu.VMEM((lon - 1, span, width), BF16),
            pltpu.VMEM((span, width), BF16),
            pltpu.SemaphoreType.DMA((count,)),
            pltpu.SemaphoreType.DMA((count,)),
        ]

    def columns(self, half):
        return pl.ds(pl.multiple_of(half * self.width, self.width), self.width)

    @staticmethod
    def stretch(owner, size):
        return pl.ds(pl.multiple_of(owner * size, size), size)

    def start_ch(self):
        other = 1 - lax.axis_index("ch")
        self.send(self.source.at[:, self.columns(other)], self.rec_ch, 0, {"ch": other})

    def start_lat(self):
        self.settle()
        own = self.source[:, self.columns(lax.axis_index("ch"))].astype(F32)
        self.part[...] = (own + self.rec_ch[...].astype(F32)).astype(BF16)
        for step in range(1, self.lat):
            peer = along("lat", step)
            rows = self.stretch(peer["lat"], self.height)
            self.send(self.part.at[rows], self.rec_lat.at[step - 1], step, peer)

    def start_lon(self):
        self.settle()
        total = self.part[self.stretch(lax.axis_index("lat"), self.height), :].astype(F32)
        for step in range(1, self.lat):
            total = total + self.rec_lat[step - 1].astype(F32)
        self.strip[...] = total.astype(BF16)
        for step in range(1, self.lon):
            peer = along("lon", step)
            source = self.strip
            if self.split:
                source = self.strip.at[self.stretch(peer["lon"], self.span)]
            self.send(source, self.rec_lon.at[step - 1], self.lat + step - 1, peer)

    def gather_lon(self):
        self.settle()
        if self.split:
            total = self.strip[self.stretch(lax.axis_index("lon"), self.span), :].astype(F32)
        else:
            total = self.strip[...].astype(F32)
        for step in range(1, self.lon):
            total = total + self.rec_lon[step - 1].astype(F32)
        self.piece[...] = total.astype(BF16)
        offset = lax.axis_index("lat") * self.height
        if self.split:
            offset = offset + lax.axis_index("lon") * self.span
        rows = pl.ds(pl.multiple_of(offset, TILE), self.span)
        self.result[rows, :] = self.piece[...]
        if self.split:
            for step in range(1, self.lon):
                slot = self.lat + self.lon - 2 + step
                self.send(self.piece, self.result.at[rows], slot, along("lon", step))

    def gather_lat(self):
        self.settle()
        rows = self.stretch(lax.axis_index("lat"), self.height)
        for step in range(1, self.lat):
            slot = self.lat + 2 * self.lon - 3 + step
            self.send(self.result.at[rows], self.result.at[rows], slot, along("lat", step))

    def finish(self):
        self.settle()


STAGES = ("start_ch", "start_lat", "start_lon", "gather_lon", "gather_lat", "finish")


class Halo(Sender):
    def __init__(self, bufs):
        super().__init__(bufs[-2:])
        self.out_side, self.out_row, self.in_side, self.in_row = bufs[:-2]

    @staticmethod
    def scratch(rows, cols, width, row_blocks):
        return [
            pltpu.VMEM((2, rows * REACH, width), BF16),
            pltpu.VMEM((row_blocks, cols, width), BF16),
            pltpu.VMEM((2, rows * REACH, width), BF16),
            pltpu.VMEM((6, cols, width), BF16),
            pltpu.SemaphoreType.DMA((8,)),
            pltpu.SemaphoreType.DMA((8,)),
        ]

    def start(self, row_block_of):
        self.send(self.out_side.at[0], self.in_side.at[1], 0, neighbour(0, -1))
        self.send(self.out_side.at[1], self.in_side.at[0], 1, neighbour(0, 1))
        slot = 2
        for row_step in (-1, 1):
            for col_step in (-1, 0, 1):
                place = (0 if row_step == 1 else 3) + 1 - col_step
                self.send(
                    self.out_row.at[row_block_of(row_step, col_step)],
                    self.in_row.at[place],
                    slot,
                    neighbour(row_step, col_step),
                )
                slot += 1


def edge_flags():
    ch_count = lax.axis_size("ch")
    bands = lax.axis_size("lat") * ch_count
    band = lax.axis_index("lat") * ch_count + lax.axis_index("ch")
    return band > 0, band < bands - 1


def extend(halo, state, ext, rows, cols):
    span = cols + 2 * REACH
    west, east = halo.in_side[0].astype(F32), halo.in_side[1].astype(F32)
    for row in range(rows):
        low, high = row * REACH, (row + 1) * REACH
        line = jnp.concatenate(
            [west[low:high], state[row * cols : (row + 1) * cols], east[low:high]], axis=0
        )
        ext[(row + 1) * span : (row + 2) * span, :] = line.astype(BF16)
    for first, row, flag in zip((0, 3), (0, rows + 1), edge_flags()):
        line = jnp.concatenate(
            [
                halo.in_row[first].astype(F32)[cols - REACH :],
                halo.in_row[first + 1].astype(F32),
                halo.in_row[first + 2].astype(F32)[:REACH],
            ],
            axis=0,
        )
        ext[row * span : (row + 1) * span, :] = jnp.where(flag, line, 0.0).astype(BF16)


def send_state(halo, state, rows, cols):
    pieces = [
        [state[r * cols : r * cols + REACH] for r in range(rows)],
        [state[(r + 1) * cols - REACH : (r + 1) * cols] for r in range(rows)],
    ]
    for side in range(2):
        halo.out_side[side] = jnp.concatenate(pieces[side], axis=0).astype(BF16)
    halo.out_row[0] = state[:cols].astype(BF16)
    halo.out_row[1] = state[(rows - 1) * cols :].astype(BF16)
    halo.start(lambda row_step, col_step: 0 if row_step == -1 else 1)


def send_spread(halo, spread, rows, cols):
    span = cols + 2 * REACH
    west = [spread[(r + 1) * span : (r + 1) * span + REACH, :] for r in range(rows)]
    east = [spread[(r + 2) * span - REACH : (r + 2) * span, :] for r in range(rows)]
    halo.out_side[0] = jnp.concatenate(west, axis=0).astype(BF16)
    halo.out_side[1] = jnp.concatenate(east, axis=0).astype(BF16)
    for block, row in enumerate((0, rows + 1)):
        base = row * span
        halo.out_row[2 * block] = spread[base + REACH : base + REACH + cols, :].astype(BF16)
        corners = [spread[base : base + REACH, :], spread[base + span - REACH : base + span, :]]
        if cols > 2 * REACH:
            corners.insert(1, jnp.zeros((cols - 2 * REACH, spread.shape[1]), F32))
        halo.out_row[2 * block + 1] = jnp.concatenate(corners, axis=0).astype(BF16)
    halo.start(
        lambda row_step, col_step: (0 if row_step == -1 else 2) + (1 if col_step else 0)
    )


def take_spread(halo, spread, gradient, rows, cols):
    span = cols + 2 * REACH
    west, east = halo.in_side[0].astype(F32), halo.in_side[1].astype(F32)
    outer = {}
    for first, row, flag in zip((0, 3), (0, rows - 1), edge_flags()):
        line = halo.in_row[first + 1].astype(F32)
        rim_west = halo.in_row[first].astype(F32)[cols - REACH :]
        rim_east = halo.in_row[first + 2].astype(F32)[:REACH]
        rims = [rim_west, rim_east]
        if cols > 2 * REACH:
            rims.insert(1, jnp.zeros((cols - 2 * REACH, line.shape[1]), F32))
        outer[row] = jnp.where(flag, line + jnp.concatenate(rims, axis=0), 0.0)
    result = []
    for row in range(rows):
        low, high = row * REACH, (row + 1) * REACH
        rims = [west[low:high], east[low:high]]
        if cols > 2 * REACH:
            rims.insert(1, jnp.zeros((cols - 2 * REACH, west.shape[1]), F32))
        base = (row + 1) * span + REACH
        line = spread[base : base + cols, :] + jnp.concatenate(rims, axis=0)
        if row in outer:
            line = line + outer[row]
        result.append(gradient[row * cols : (row + 1) * cols].astype(F32) + line)
    return result


def aligned(index, size):
    return pl.ds(pl.multiple_of(index * size, size), size)


GROUP = 4


def over_rows(rows, body):
    group = GROUP if rows % GROUP == 0 else 1

    def step(index, carry):
        for inner in range(group):
            body(index * group + inner)
        return carry

    lax.fori_loop(0, rows // group, step, 0)


def make_bands(base, bands, rows, cols, basis_count):
    width = base.shape[1]

    def one(row):
        table = base[aligned(row, 2 * basis_count), :]
        for k in range(basis_count):
            line = jnp.broadcast_to(table[k : k + 1], (cols, width))
            moved = pltpu.roll(line, 0, 1, stride=1, stride_axis=0)
            start = pl.multiple_of((row * basis_count + k) * cols, cols)
            bands[pl.ds(start, cols), :] = moved.astype(BF16)

    over_rows(rows, one)


def stencil(bands, ext, features, rows, cols, basis_count):
    span = cols + 2 * REACH
    channels = ext.shape[1]

    def one(row):
        lhs = bands[aligned(row, basis_count * cols), :][:, : 3 * span]
        rhs = ext[pl.ds(pl.multiple_of(row * span, span), 3 * span), :]
        out = jnp.dot(lhs, rhs, preferred_element_type=F32).astype(BF16)
        for k in range(basis_count):
            features[aligned(row, cols), k * channels : (k + 1) * channels] = out[
                k * cols : (k + 1) * cols
            ]

    over_rows(rows, one)


def adjoint(bands, errs, spread, rows, cols, basis_count):
    span = cols + 2 * REACH
    spread[...] = jnp.zeros_like(spread)

    def one(row):
        lhs = bands[aligned(row, basis_count * cols), :][:, : 3 * span]
        rhs = errs[aligned(row, basis_count * cols), :]
        out = lax.dot_general(lhs, rhs, (((0,), (0,)), ((), ())), preferred_element_type=F32)
        place = pl.ds(pl.multiple_of(row * span, span), 3 * span)
        spread[place, :] = spread[place, :] + out

    over_rows(rows, one)


def rows_product(left, right):
    return lax.dot_general(left, right, (((0,), (0,)), ((), ())), preferred_element_type=F32)


def net_kernel(plan, *refs):
    rows, cols, basis_count, layers = plan
    latent_in, encoder_weight, base, weights, cotangent = refs[:5]
    state_out, latent_grad = refs[5:7]
    results = refs[7 : 8 + layers]
    rest = list(refs[8 + layers :])
    bands, ext, spread, errs, features, preact = rest[:6]
    rest = rest[6:]
    halos = []
    for _ in range(2 * layers):
        halos.append(Halo(rest[:6]))
        rest = rest[6:]
    sums = []
    for index in range(layers + 1):
        sums.append(GradSum(results[index], rest[:9]))
        rest = rest[9:]
    channels = ext.shape[1]
    progress = [0] * (layers + 1)

    def advance(index):
        getattr(sums[index], STAGES[progress[index]])()
        progress[index] += 1

    greet()
    state = jnp.dot(latent_in[...], encoder_weight[...], preferred_element_type=F32)
    state = state.astype(BF16).astype(F32)
    for layer in range(layers):
        send_state(halos[layer], state, rows, cols)
        if layer == 0:
            make_bands(base, bands, rows, cols, basis_count)
        halos[layer].settle()
        extend(halos[layer], state, ext, rows, cols)
        stencil(bands, ext, features.at[layer], rows, cols, basis_count)
        pre = jnp.dot(features[layer], weights[layer], preferred_element_type=F32)
        preact[layer] = pre
        state = (state + pre / (1.0 + jnp.exp(-pre))).astype(BF16).astype(F32)
    state_out[...] = state.astype(BF16)

    gradient = cotangent[...].astype(F32)
    for layer in reversed(range(layers)):
        pre = preact[layer]
        sigma = 1.0 / (1.0 + jnp.exp(-pre))
        act_grad = (gradient * sigma * (1.0 + pre * (1.0 - sigma))).astype(BF16)
        for k in range(basis_count):
            block = weights[layer, k * channels : (k + 1) * channels, :]
            out = lax.dot_general(
                act_grad, block, (((1,), (1,)), ((), ())), preferred_element_type=F32
            ).astype(BF16)
            for row in range(rows):
                start = (row * basis_count + k) * cols
                errs[start : start + cols, :] = out[row * cols : (row + 1) * cols]
        adjoint(bands, errs, spread, rows, cols, basis_count)
        halo = halos[layers + layer]
        send_spread(halo, spread, rows, cols)
        sums[layer].source[...] = rows_product(features[layer], act_grad).astype(BF16)
        advance(layer)
        if layer + 1 < layers:
            advance(layer + 1)
        halo.settle()
        lines = take_spread(halo, spread, gradient, rows, cols)
        gradient = jnp.concatenate(lines, axis=0).astype(BF16).astype(F32)
    latent_grad[...] = gradient.astype(BF16)
    sums[layers].source[...] = rows_product(latent_in[...], gradient.astype(BF16)).astype(BF16)
    advance(layers)
    while min(progress) < len(STAGES):
        for index in list(range(layers))[::-1] + [layers]:
            if progress[index] < len(STAGES):
                advance(index)


def run_net(plan, sizes, latent_in, encoder_weight, base, weights, cotangent):
    rows, cols, basis_count, layers = plan
    cells, channels = rows * cols, weights.shape[2]
    features = basis_count * channels
    span = cols + 2 * REACH
    in_features = encoder_weight.shape[0]
    heights = [features] * layers + [in_features]
    scratch = [
        pltpu.VMEM((rows * basis_count * cols, base.shape[1]), BF16),
        pltpu.VMEM(((rows + 2) * span, channels), BF16),
        pltpu.VMEM(((rows + 2) * span, channels), F32),
        pltpu.VMEM((rows * basis_count * cols, channels), BF16),
        pltpu.VMEM((layers, cells, features), BF16),
        pltpu.VMEM((layers, cells, channels), F32),
    ]
    for index in range(2 * layers):
        scratch += Halo.scratch(rows, cols, channels, 2 if index < layers else 4)
    for height in heights:
        scratch += GradSum.scratch(sizes, height, channels)
    vmem = pl.BlockSpec(memory_space=pltpu.VMEM)
    field = jax.ShapeDtypeStruct((cells, channels), BF16)
    grads = [jax.ShapeDtypeStruct((height, channels // 2), BF16) for height in heights]
    return pl.pallas_call(
        functools.partial(net_kernel, plan),
        out_shape=[field, field] + grads,
        in_specs=[vmem] * 5,
        out_specs=[vmem] * (3 + layers),
        scratch_shapes=scratch,
        compiler_params=pltpu.CompilerParams(
            collective_id=0, has_side_effects=True, vmem_limit_bytes=56 << 20
        ),
    )(latent_in, encoder_weight, base, weights, cotangent)


def from_behind(block, axis, distance):
    devices = range(lax.axis_size(axis))
    route = [(i - distance, i) for i in devices if i - distance in devices]
    return lax.ppermute(block, axis, route)


def padded(block, sides, width, periodic):
    for axis, dim in sides:
        count = lax.axis_size(axis)
        forward = [(i, i + 1) for i in range(count - 1)]
        if periodic:
            forward.append((count - 1, 0))
        backward = [(target, source) for source, target in forward]
        low = lax.ppermute(
            lax.slice_in_dim(block, block.shape[dim] - width, None, axis=dim), axis, forward
        )
        high = lax.ppermute(lax.slice_in_dim(block, 0, width, axis=dim), axis, backward)
        block = jnp.concatenate([low, block, high], axis=dim)
    return block


def add_edges(middle, to_first, to_last):
    row_count = middle.shape[0]
    rest_pads = [(0, 0)] * (middle.ndim - 1)
    lower = jnp.pad(to_first, [(0, row_count - 1)] + rest_pads)
    upper = jnp.pad(to_last, [(row_count - 1, 0)] + rest_pads)
    return middle + lower + upper


def per_device(
    input_field,
    encoder_filter,
    row_owner,
    encoder_weight,
    disco_basis,
    row_widths,
    block_weights,
    cotangent,
):
    rows_in, cols_in, in_width = input_field.shape
    rows_dev = rows_in // 2
    cols_dev = cols_in // 2
    basis_count = encoder_filter.shape[1]
    tap_count = encoder_filter.shape[2]
    channels = block_weights.shape[2]
    layers = block_weights.shape[0]
    cell_count = rows_dev * cols_dev
    extended_in = padded(input_field, (("lon", 1),), TAP_REACH, True)
    filter_values = encoder_filter.astype(jnp.float32)
    accumulated = jnp.zeros((rows_in, cols_dev, basis_count, in_width), jnp.float32)
    for tap_index in range(tap_count):
        sampled = extended_in[:, tap_index : tap_index + cols_in : 2, :]
        accumulated = (
            accumulated
            + sampled[:, :, None, :].astype(jnp.float32)
            * filter_values[:, None, :, tap_index, None]
        )
    filtered_in = accumulated.astype(jnp.bfloat16).reshape(
        rows_in, cols_dev * basis_count * in_width
    )
    first_row = lax.axis_index(("lat", "ch")) * rows_dev
    relative = row_owner - first_row + 1
    selector = (relative[None, :] == jnp.arange(rows_dev + 2, dtype=jnp.int32)[:, None]).astype(
        jnp.bfloat16
    )
    summed = jnp.dot(selector, filtered_in, preferred_element_type=jnp.float32)
    from_above = from_behind(summed[0:1].astype(jnp.bfloat16), ("lat", "ch"), -1).astype(
        jnp.float32
    )
    from_below = from_behind(summed[rows_dev + 1 :].astype(jnp.bfloat16), ("lat", "ch"), 1).astype(
        jnp.float32
    )
    regridded = add_edges(summed[1 : rows_dev + 1], from_below, from_above)
    latent_in = regridded.astype(jnp.bfloat16).reshape(cell_count, basis_count * in_width)
    offsets = jnp.abs(jnp.arange(2 * REACH + 1, dtype=jnp.int32) - REACH)
    keep = offsets[None, :] <= row_widths[:, None]
    masked = jnp.where(keep[:, None, None, :], disco_basis, jnp.zeros_like(disco_basis))
    span = cols_dev + 2 * REACH
    table = jnp.pad(masked, ((0, 0), (0, basis_count), (0, 0), (0, span - masked.shape[3])))
    table = table.reshape(rows_dev * 2 * basis_count, 3 * span).astype(jnp.float32)
    lanes = -(-3 * span // 128) * 128
    table = jnp.pad(table, ((0, 0), (0, lanes - 3 * span)))
    own_width = channels // lax.axis_size("ch")
    sizes = (lax.axis_size("lat"), lax.axis_size("lon"))
    plan = (rows_dev, cols_dev, basis_count, layers)
    outs = run_net(
        plan,
        sizes,
        latent_in,
        encoder_weight,
        table,
        block_weights,
        cotangent.reshape(cell_count, channels),
    )
    current, gradient = (field.reshape(rows_dev, cols_dev, channels) for field in outs[:2])
    sums = [value.astype(jnp.float32) for value in outs[2:]]
    block_sum, encoder_sum = jnp.stack(sums[:-1]), sums[-1]
    cells_total = cell_count * lax.axis_size("lon") * lax.axis_size(("lat", "ch"))
    normalizer = 1.0 / math.sqrt(cells_total)
    block_grads = (block_sum * normalizer).reshape(layers, basis_count * channels, own_width)
    encoder_grad = encoder_sum * normalizer
    return (current, gradient, block_grads, encoder_grad)


def solution(mesh):
    placed = (
        P(("ens", "lat", "ch"), "lon", None),
        P(("lat", "ch"), None, None),
        P(("ens", "lat", "ch")),
        P(),
        P(("lat", "ch"), None, None, None),
        P(("lat", "ch")),
        P(),
        P(("ens", "lat", "ch"), "lon", None),
    )
    return jax.shard_map(
        per_device,
        mesh=mesh,
        in_specs=placed,
        out_specs=(
            P(("ens", "lat", "ch"), "lon", None),
            P(("ens", "lat", "ch"), "lon", None),
            P("ens", None, "ch"),
            P("ens", "ch"),
        ),
        check_vma=False,
    )
```

```python
import functools
import math

import jax
import jax.numpy as jnp
from jax import lax
from jax.experimental import pallas as pl
from jax.experimental.pallas import tpu as pltpu
from jax.sharding import PartitionSpec as P

REACH = 8
TAP_REACH = 2
TILE = 16
MESH = pl.DeviceIdType.MESH
BF16 = jnp.bfloat16
F32 = jnp.float32


def along(axis, steps):
    count = lax.axis_size(axis)
    return {axis: lax.rem(lax.axis_index(axis) + steps + count, count)}


def neighbour(row_step, col_step):
    ch_count = lax.axis_size("ch")
    bands = lax.axis_size("lat") * ch_count
    band = lax.axis_index("lat") * ch_count + lax.axis_index("ch")
    band = lax.rem(band + row_step + bands, bands)
    target = {}
    if row_step:
        target = {"lat": band // ch_count, "ch": lax.rem(band, ch_count)}
    if col_step:
        target.update(along("lon", col_step))
    return target


AROUND = [(r, c) for r in (-1, 0, 1) for c in (-1, 0, 1) if r or c]


def greet():
    targets = [neighbour(r, c) for r, c in AROUND]
    for axis in ("ch", "lat", "lon"):
        targets += [along(axis, step) for step in range(1, lax.axis_size(axis))]
    barrier = pltpu.get_barrier_semaphore()
    for target in targets:
        pl.semaphore_signal(barrier, inc=1, device_id=target, device_id_type=MESH)
    pl.semaphore_wait(barrier, len(targets))


class Sender:
    def __init__(self, sems):
        self.ssem, self.rsem = sems
        self.pending = []

    def send(self, source, target, slot, device):
        copy = pltpu.make_async_remote_copy(
            src_ref=source,
            dst_ref=target,
            send_sem=self.ssem.at[slot],
            recv_sem=self.rsem.at[slot],
            device_id=device,
            device_id_type=MESH,
        )
        copy.start()
        self.pending.append(copy)

    def settle(self):
        for copy in self.pending:
            copy.wait()
        self.pending = []


class GradSum(Sender):
    def __init__(self, result, bufs):
        super().__init__(bufs[-2:])
        self.result = result
        self.source, self.rec_ch, self.part, self.rec_lat, self.strip, self.rec_pair, self.half, self.rec_far, self.piece = bufs[:-2]
        self.width = self.part.shape[1]
        self.lat, self.lon = lax.axis_size("lat"), lax.axis_size("lon")
        self.height = self.strip.shape[0]
        self.span = self.piece.shape[0]
        self.pair = self.height // self.span
        self.far = self.lon // self.pair
        self.side = lax.rem(lax.axis_index("lon"), self.pair)

    @staticmethod
    def scratch(sizes, rows, columns):
        lat, lon = sizes
        width = columns // 2
        height = rows // lat
        pair = 2 if lon % 2 == 0 and height % (2 * TILE) == 0 else 1
        span, far = height // pair, lon // pair
        count = 1 + 2 * (lat - 1) + 2 * (pair - 1) + far - 1
        return [
            pltpu.VMEM((rows, columns), BF16),
            pltpu.VMEM((rows, width), BF16),
            pltpu.VMEM((rows, width), BF16),
            pltpu.VMEM((lat - 1, height, width), BF16),
            pltpu.VMEM((height, width), BF16),
            pltpu.VMEM((span, width), BF16),
            pltpu.VMEM((span, width), BF16),
            pltpu.VMEM((far - 1, span, width), BF16),
            pltpu.VMEM((span, width), BF16),
            pltpu.SemaphoreType.DMA((count,)),
            pltpu.SemaphoreType.DMA((count,)),
        ]

    def columns(self, half):
        return pl.ds(pl.multiple_of(half * self.width, self.width), self.width)

    @staticmethod
    def stretch(owner, size):
        return pl.ds(pl.multiple_of(owner * size, size), size)

    def start_ch(self):
        other = 1 - lax.axis_index("ch")
        self.send(self.source.at[:, self.columns(other)], self.rec_ch, 0, {"ch": other})

    def start_lat(self):
        self.settle()
        own = self.source[:, self.columns(lax.axis_index("ch"))].astype(F32)
        self.part[...] = (own + self.rec_ch[...].astype(F32)).astype(BF16)
        for step in range(1, self.lat):
            peer = along("lat", step)
            rows = self.stretch(peer["lat"], self.height)
            self.send(self.part.at[rows], self.rec_lat.at[step - 1], step, peer)

    def start_lon(self):
        self.settle()
        total = self.part[self.stretch(lax.axis_index("lat"), self.height), :].astype(F32)
        for step in range(1, self.lat):
            total = total + self.rec_lat[step - 1].astype(F32)
        self.strip[...] = total.astype(BF16)
        if self.pair > 1:
            rows = self.stretch(1 - self.side, self.span)
            self.send(self.strip.at[rows], self.rec_pair, self.lat, along("lon", 1 - 2 * self.side))

    def start_far(self):
        self.settle()
        total = self.strip[self.stretch(self.side, self.span), :].astype(F32)
        if self.pair > 1:
            total = total + self.rec_pair[...].astype(F32)
        self.half[...] = total.astype(BF16)
        for step in range(1, self.far):
            self.send(
                self.half, self.rec_far.at[step - 1], self.lat + step, along("lon", self.pair * step)
            )

    def gather_lon(self):
        self.settle()
        total = self.half[...].astype(F32)
        for step in range(1, self.far):
            total = total + self.rec_far[step - 1].astype(F32)
        self.piece[...] = total.astype(BF16)
        offset = lax.axis_index("lat") * self.height + self.side * self.span
        rows = pl.ds(pl.multiple_of(offset, TILE), self.span)
        self.result[rows, :] = self.piece[...]
        if self.pair > 1:
            slot = self.lat + self.far
            self.send(self.piece, self.result.at[rows], slot, along("lon", 1 - 2 * self.side))

    def gather_lat(self):
        self.settle()
        rows = self.stretch(lax.axis_index("lat"), self.height)
        for step in range(1, self.lat):
            slot = self.lat + self.far + self.pair - 2 + step
            self.send(self.result.at[rows], self.result.at[rows], slot, along("lat", step))

    def finish(self):
        self.settle()


STAGES = ("start_ch", "start_lat", "start_lon", "start_far", "gather_lon", "gather_lat", "finish")


class Halo(Sender):
    def __init__(self, bufs):
        super().__init__(bufs[-2:])
        self.out_side, self.out_row, self.in_side, self.in_row = bufs[:-2]

    @staticmethod
    def scratch(rows, cols, width, row_blocks):
        return [
            pltpu.VMEM((2, rows * REACH, width), BF16),
            pltpu.VMEM((row_blocks, cols, width), BF16),
            pltpu.VMEM((2, rows * REACH, width), BF16),
            pltpu.VMEM((6, cols, width), BF16),
            pltpu.SemaphoreType.DMA((8,)),
            pltpu.SemaphoreType.DMA((8,)),
        ]

    def start(self, row_block_of):
        self.send(self.out_side.at[0], self.in_side.at[1], 0, neighbour(0, -1))
        self.send(self.out_side.at[1], self.in_side.at[0], 1, neighbour(0, 1))
        slot = 2
        for row_step in (-1, 1):
            for col_step in (-1, 0, 1):
                place = (0 if row_step == 1 else 3) + 1 - col_step
                self.send(
                    self.out_row.at[row_block_of(row_step, col_step)],
                    self.in_row.at[place],
                    slot,
                    neighbour(row_step, col_step),
                )
                slot += 1


def edge_flags():
    ch_count = lax.axis_size("ch")
    bands = lax.axis_size("lat") * ch_count
    band = lax.axis_index("lat") * ch_count + lax.axis_index("ch")
    return band > 0, band < bands - 1


def extend(halo, state, ext, rows, cols):
    span = cols + 2 * REACH
    west, east = halo.in_side[0].astype(F32), halo.in_side[1].astype(F32)
    for row in range(rows):
        low, high = row * REACH, (row + 1) * REACH
        line = jnp.concatenate(
            [west[low:high], state[row * cols : (row + 1) * cols], east[low:high]], axis=0
        )
        ext[(row + 1) * span : (row + 2) * span, :] = line.astype(BF16)
    for first, row, flag in zip((0, 3), (0, rows + 1), edge_flags()):
        line = jnp.concatenate(
            [
                halo.in_row[first].astype(F32)[cols - REACH :],
                halo.in_row[first + 1].astype(F32),
                halo.in_row[first + 2].astype(F32)[:REACH],
            ],
            axis=0,
        )
        ext[row * span : (row + 1) * span, :] = jnp.where(flag, line, 0.0).astype(BF16)


def send_state(halo, state, rows, cols):
    pieces = [
        [state[r * cols : r * cols + REACH] for r in range(rows)],
        [state[(r + 1) * cols - REACH : (r + 1) * cols] for r in range(rows)],
    ]
    for side in range(2):
        halo.out_side[side] = jnp.concatenate(pieces[side], axis=0).astype(BF16)
    halo.out_row[0] = state[:cols].astype(BF16)
    halo.out_row[1] = state[(rows - 1) * cols :].astype(BF16)
    halo.start(lambda row_step, col_step: 0 if row_step == -1 else 1)


def send_spread(halo, spread, rows, cols):
    span = cols + 2 * REACH
    west = [spread[(r + 1) * span : (r + 1) * span + REACH, :] for r in range(rows)]
    east = [spread[(r + 2) * span - REACH : (r + 2) * span, :] for r in range(rows)]
    halo.out_side[0] = jnp.concatenate(west, axis=0).astype(BF16)
    halo.out_side[1] = jnp.concatenate(east, axis=0).astype(BF16)
    for block, row in enumerate((0, rows + 1)):
        base = row * span
        halo.out_row[2 * block] = spread[base + REACH : base + REACH + cols, :].astype(BF16)
        corners = [spread[base : base + REACH, :], spread[base + span - REACH : base + span, :]]
        if cols > 2 * REACH:
            corners.insert(1, jnp.zeros((cols - 2 * REACH, spread.shape[1]), F32))
        halo.out_row[2 * block + 1] = jnp.concatenate(corners, axis=0).astype(BF16)
    halo.start(
        lambda row_step, col_step: (0 if row_step == -1 else 2) + (1 if col_step else 0)
    )


def take_spread(halo, spread, gradient, rows, cols):
    span = cols + 2 * REACH
    west, east = halo.in_side[0].astype(F32), halo.in_side[1].astype(F32)
    outer = {}
    for first, row, flag in zip((0, 3), (0, rows - 1), edge_flags()):
        line = halo.in_row[first + 1].astype(F32)
        rim_west = halo.in_row[first].astype(F32)[cols - REACH :]
        rim_east = halo.in_row[first + 2].astype(F32)[:REACH]
        rims = [rim_west, rim_east]
        if cols > 2 * REACH:
            rims.insert(1, jnp.zeros((cols - 2 * REACH, line.shape[1]), F32))
        outer[row] = jnp.where(flag, line + jnp.concatenate(rims, axis=0), 0.0)
    result = []
    for row in range(rows):
        low, high = row * REACH, (row + 1) * REACH
        rims = [west[low:high], east[low:high]]
        if cols > 2 * REACH:
            rims.insert(1, jnp.zeros((cols - 2 * REACH, west.shape[1]), F32))
        base = (row + 1) * span + REACH
        line = spread[base : base + cols, :] + jnp.concatenate(rims, axis=0)
        if row in outer:
            line = line + outer[row]
        result.append(gradient[row * cols : (row + 1) * cols].astype(F32) + line)
    return result


def aligned(index, size):
    return pl.ds(pl.multiple_of(index * size, size), size)


GROUP = 4


def over_rows(rows, body):
    group = GROUP if rows % GROUP == 0 else 1

    def step(index, carry):
        for inner in range(group):
            body(index * group + inner)
        return carry

    lax.fori_loop(0, rows // group, step, 0)


def make_bands(base, bands, rows, cols, basis_count):
    width = base.shape[1]

    def one(row):
        table = base[aligned(row, 2 * basis_count), :]
        for k in range(basis_count):
            line = jnp.broadcast_to(table[k : k + 1], (cols, width))
            moved = pltpu.roll(line, 0, 1, stride=1, stride_axis=0)
            start = pl.multiple_of((row * basis_count + k) * cols, cols)
            bands[pl.ds(start, cols), :] = moved.astype(BF16)

    over_rows(rows, one)


def stencil(bands, ext, features, rows, cols, basis_count):
    span = cols + 2 * REACH
    channels = ext.shape[1]

    def one(row):
        lhs = bands[aligned(row, basis_count * cols), :][:, : 3 * span]
        rhs = ext[pl.ds(pl.multiple_of(row * span, span), 3 * span), :]
        out = jnp.dot(lhs, rhs, preferred_element_type=F32).astype(BF16)
        for k in range(basis_count):
            features[aligned(row, cols), k * channels : (k + 1) * channels] = out[
                k * cols : (k + 1) * cols
            ]

    over_rows(rows, one)


def adjoint(bands, errs, spread, rows, cols, basis_count):
    span = cols + 2 * REACH
    spread[...] = jnp.zeros_like(spread)

    def one(row):
        lhs = bands[aligned(row, basis_count * cols), :][:, : 3 * span]
        rhs = errs[aligned(row, basis_count * cols), :]
        out = lax.dot_general(lhs, rhs, (((0,), (0,)), ((), ())), preferred_element_type=F32)
        place = pl.ds(pl.multiple_of(row * span, span), 3 * span)
        spread[place, :] = spread[place, :] + out

    over_rows(rows, one)


def rows_product(left, right):
    return lax.dot_general(left, right, (((0,), (0,)), ((), ())), preferred_element_type=F32)
TAPS_LEFT = TAP_REACH


class InputHalo(Sender):
    def __init__(self, bufs):
        super().__init__(bufs[-2:])
        (
            self.edges,
            self.out_cols,
            self.out_table,
            self.in_cols,
            self.in_row,
            self.in_table,
            self.in_tile,
        ) = bufs[:-2]

    @staticmethod
    def scratch(rows_in, cols_in, width, table_rows, lanes):
        return [
            pltpu.VMEM((3, rows_in, width), F32),
            pltpu.VMEM((3, rows_in, width), BF16),
            pltpu.VMEM((2, table_rows, lanes), F32),
            pltpu.VMEM((3, rows_in, width), BF16),
            pltpu.VMEM((2, cols_in, width), BF16),
            pltpu.VMEM((2, table_rows, lanes), F32),
            pltpu.VMEM((4, TILE, width), BF16),
            pltpu.SemaphoreType.DMA((10,)),
            pltpu.SemaphoreType.DMA((10,)),
        ]

    def start(self, field, table, owner, rows_in, cols_in):
        first = own_first_row(rows_in // 2)
        table_rows = self.out_table.shape[1]
        for block, row, target in ((0, 0, first - 1), (1, rows_in - 1, first + rows_in // 2)):
            feeds = jnp.where(owner[row] == target, 1.0, 0.0)
            self.out_table[block] = table[row * table_rows : (row + 1) * table_rows, :] * feeds
        last = (rows_in - 1) * cols_in
        lines = (field.at[pl.ds(0, cols_in)], field.at[pl.ds(last, cols_in)])
        slot = 0
        for block, row_step in ((0, -1), (1, 1)):
            self.send(lines[block], self.in_row.at[1 - block], slot, neighbour(row_step, 0))
            base = block * last
            west = field.at[pl.ds(base, TILE)]
            east = field.at[pl.ds(base + cols_in - TILE, TILE)]
            place = 2 * (1 - block)
            self.send(west, self.in_tile.at[place + 1], slot + 1, neighbour(row_step, -1))
            self.send(east, self.in_tile.at[place], slot + 2, neighbour(row_step, 1))
            slot += 3

        def one(row):
            low = field[pl.ds(pl.multiple_of(row * cols_in, TILE), TILE), :].astype(F32)
            start = pl.multiple_of(row * cols_in + cols_in - TILE, TILE)
            high = field[pl.ds(start, TILE), :].astype(F32)
            self.edges[0, pl.ds(row, 1), :] = high[TILE - 2 : TILE - 1]
            self.edges[1, pl.ds(row, 1), :] = high[TILE - 1 : TILE]
            self.edges[2, pl.ds(row, 1), :] = low[0:1]

        over_rows(rows_in, one)
        self.out_cols[...] = self.edges[...].astype(BF16)
        self.send(self.out_cols.at[pl.ds(0, 2)], self.in_cols.at[pl.ds(0, 2)], 6, neighbour(0, 1))
        self.send(self.out_cols.at[2], self.in_cols.at[2], 7, neighbour(0, -1))
        self.send(self.out_table.at[0], self.in_table.at[1], 8, neighbour(-1, 0))
        self.send(self.out_table.at[1], self.in_table.at[0], 9, neighbour(1, 0))


def own_first_row(rows):
    return (lax.axis_index("lat") * lax.axis_size("ch") + lax.axis_index("ch")) * rows


def tap_matrix(table, basis_count, cols, cols_in):
    lanes = table.shape[1]
    blocks = []
    for k in range(basis_count):
        line = jnp.broadcast_to(table[k : k + 1], (cols, lanes))
        moved = pltpu.roll(line, 0, 1, stride=2, stride_axis=0)
        wrapped = pltpu.roll(moved, cols_in + TILE - TAPS_LEFT, 1)
        moved = pltpu.roll(moved, lanes - TAPS_LEFT, 1)
        lane = lax.broadcasted_iota(jnp.int32, (cols, lanes), 1)
        at_end = (lane >= cols_in + TILE - TAPS_LEFT) & (lane < cols_in + TILE)
        blocks.append(jnp.where(at_end, wrapped, moved))
    return jnp.concatenate(blocks, axis=0)[:, : cols_in + TILE].astype(BF16)


def filtered_row(table, line, left_two, left_one, right, basis_count, cols, cols_in):
    width = line.shape[1]
    place = lax.broadcasted_iota(jnp.int32, (TILE, width), 0)
    tile = jnp.where(place == 0, jnp.broadcast_to(right, (TILE, width)), 0.0)
    tile = jnp.where(place == TILE - 2, jnp.broadcast_to(left_two, (TILE, width)), tile)
    tile = jnp.where(place == TILE - 1, jnp.broadcast_to(left_one, (TILE, width)), tile)
    rhs = jnp.concatenate([line, tile.astype(BF16)], axis=0)
    lhs = tap_matrix(table, basis_count, cols, cols_in)
    return jnp.dot(lhs, rhs, preferred_element_type=F32).astype(BF16)


def finish_encode(halo, field, table, owner, filtered, latent_in, plan, rows_in, cols_in):
    rows, cols, basis_count, _ = plan
    table_rows = halo.out_table.shape[1]
    block = basis_count * cols
    width = field.shape[1]
    halo.settle()
    halo.edges[...] = halo.in_cols[...].astype(F32)

    def one(row):
        sides = [halo.edges[index, pl.ds(row, 1), :] for index in range(3)]
        line = field[aligned(row, cols_in), :]
        taps = table[aligned(row, table_rows), :]
        filtered[aligned(row + 1, block), :] = filtered_row(
            taps, line, *sides, basis_count, cols, cols_in
        )

    over_rows(rows_in, one)
    for side, row in ((0, 0), (1, rows_in + 1)):
        west = halo.in_tile[2 * side].astype(F32)
        east = halo.in_tile[2 * side + 1].astype(F32)
        filtered[row * block : (row + 1) * block, :] = filtered_row(
            halo.in_table[side],
            halo.in_row[side],
            west[TILE - 2 : TILE - 1],
            west[TILE - 1 : TILE],
            east[0:1],
            basis_count,
            cols,
            cols_in,
        )
    first = own_first_row(rows)
    for row in range(rows):
        total = None
        for offset in range(-1, 3):
            source = 2 * row + offset
            term = filtered[(source + 1) * block : (source + 2) * block, :].astype(F32)
            if 0 <= source < rows_in:
                term = term * jnp.where(owner[source] == first + row, 1.0, 0.0)
            total = term if total is None else total + term
        total = total.astype(BF16)
        for k in range(basis_count):
            latent_in[row * cols : (row + 1) * cols, k * width : (k + 1) * width] = total[
                k * cols : (k + 1) * cols
            ]


def lanes_of(count):
    return -(-(count + 2 * TILE) // 128) * 128


def net_kernel(plan, *refs):
    rows, cols, basis_count, layers = plan
    field, table, owner, encoder_weight, base, weights, cotangent = refs[:7]
    state_out, latent_grad = refs[7:9]
    results = refs[9 : 10 + layers]
    rest = list(refs[10 + layers :])
    bands, ext, spread, errs, features, preact, filtered, latent_in = rest[:8]
    input_halo = InputHalo(rest[8:17])
    rest = rest[17:]
    halos = []
    for _ in range(2 * layers):
        halos.append(Halo(rest[:6]))
        rest = rest[6:]
    sums = []
    for index in range(layers + 1):
        sums.append(GradSum(results[index], rest[:11]))
        rest = rest[11:]
    channels = ext.shape[1]
    progress = [0] * (layers + 1)

    def advance(index):
        getattr(sums[index], STAGES[progress[index]])()
        progress[index] += 1

    greet()
    rows_in = owner.shape[0]
    cols_in = field.shape[0] // rows_in
    input_halo.start(field, table, owner, rows_in, cols_in)
    make_bands(base, bands, rows, cols, basis_count)
    finish_encode(input_halo, field, table, owner, filtered, latent_in, plan, rows_in, cols_in)
    state = jnp.dot(latent_in[...], encoder_weight[...], preferred_element_type=F32)
    state = state.astype(BF16).astype(F32)
    for layer in range(layers):
        send_state(halos[layer], state, rows, cols)
        halos[layer].settle()
        extend(halos[layer], state, ext, rows, cols)
        stencil(bands, ext, features.at[layer], rows, cols, basis_count)
        pre = jnp.dot(features[layer], weights[layer], preferred_element_type=F32)
        preact[layer] = pre
        state = (state + pre / (1.0 + jnp.exp(-pre))).astype(BF16).astype(F32)
    state_out[...] = state.astype(BF16)

    gradient = cotangent[...].astype(F32)
    for layer in reversed(range(layers)):
        pre = preact[layer]
        sigma = 1.0 / (1.0 + jnp.exp(-pre))
        act_grad = (gradient * sigma * (1.0 + pre * (1.0 - sigma))).astype(BF16)
        for k in range(basis_count):
            block = weights[layer, k * channels : (k + 1) * channels, :]
            out = lax.dot_general(
                act_grad, block, (((1,), (1,)), ((), ())), preferred_element_type=F32
            ).astype(BF16)
            for row in range(rows):
                start = (row * basis_count + k) * cols
                errs[start : start + cols, :] = out[row * cols : (row + 1) * cols]
        adjoint(bands, errs, spread, rows, cols, basis_count)
        halo = halos[layers + layer]
        send_spread(halo, spread, rows, cols)
        sums[layer].source[...] = rows_product(features[layer], act_grad).astype(BF16)
        advance(layer)
        if layer + 1 < layers:
            advance(layer + 1)
        halo.settle()
        lines = take_spread(halo, spread, gradient, rows, cols)
        gradient = jnp.concatenate(lines, axis=0).astype(BF16).astype(F32)
    latent_grad[...] = gradient.astype(BF16)
    sums[layers].source[...] = rows_product(latent_in[...], gradient.astype(BF16)).astype(BF16)
    advance(layers)
    while min(progress) < len(STAGES):
        for index in list(range(layers))[::-1] + [layers]:
            if progress[index] < len(STAGES):
                advance(index)


def run_net(plan, sizes, field_in, table, owner, encoder_weight, base, weights, cotangent):
    rows, cols, basis_count, layers = plan
    cells, channels = rows * cols, weights.shape[2]
    features = basis_count * channels
    span = cols + 2 * REACH
    rows_in = owner.shape[0]
    in_features = encoder_weight.shape[0]
    heights = [features] * layers + [in_features]
    scratch = [
        pltpu.VMEM((rows * basis_count * cols, base.shape[1]), BF16),
        pltpu.VMEM(((rows + 2) * span, channels), BF16),
        pltpu.VMEM(((rows + 2) * span, channels), F32),
        pltpu.VMEM((rows * basis_count * cols, channels), BF16),
        pltpu.VMEM((layers, cells, features), BF16),
        pltpu.VMEM((layers, cells, channels), F32),
        pltpu.VMEM(((rows_in + 2) * basis_count * cols, field_in.shape[1]), BF16),
        pltpu.VMEM((cells, in_features), BF16),
    ]
    scratch += InputHalo.scratch(
        rows_in, field_in.shape[0] // rows_in, field_in.shape[1], table.shape[0] // rows_in, table.shape[1]
    )
    for index in range(2 * layers):
        scratch += Halo.scratch(rows, cols, channels, 2 if index < layers else 4)
    for height in heights:
        scratch += GradSum.scratch(sizes, height, channels)
    vmem = pl.BlockSpec(memory_space=pltpu.VMEM)
    field = jax.ShapeDtypeStruct((cells, channels), BF16)
    grads = [jax.ShapeDtypeStruct((height, channels // 2), BF16) for height in heights]
    return pl.pallas_call(
        functools.partial(net_kernel, plan),
        out_shape=[field, field] + grads,
        in_specs=[vmem, vmem, pl.BlockSpec(memory_space=pltpu.SMEM)] + [vmem] * 4,
        out_specs=[vmem] * (3 + layers),
        scratch_shapes=scratch,
        compiler_params=pltpu.CompilerParams(
            collective_id=0, has_side_effects=True, vmem_limit_bytes=56 << 20
        ),
    )(field_in, table, owner, encoder_weight, base, weights, cotangent)


def per_device(
    input_field,
    encoder_filter,
    row_owner,
    encoder_weight,
    disco_basis,
    row_widths,
    block_weights,
    cotangent,
):
    rows_in, cols_in, in_width = input_field.shape
    rows_dev = rows_in // 2
    cols_dev = cols_in // 2
    basis_count = encoder_filter.shape[1]
    tap_count = encoder_filter.shape[2]
    channels = block_weights.shape[2]
    layers = block_weights.shape[0]
    cell_count = rows_dev * cols_dev
    offsets = jnp.abs(jnp.arange(2 * REACH + 1, dtype=jnp.int32) - REACH)
    keep = offsets[None, :] <= row_widths[:, None]
    masked = jnp.where(keep[:, None, None, :], disco_basis, jnp.zeros_like(disco_basis))
    span = cols_dev + 2 * REACH
    table = jnp.pad(masked, ((0, 0), (0, basis_count), (0, 0), (0, span - masked.shape[3])))
    table = table.reshape(rows_dev * 2 * basis_count, 3 * span).astype(jnp.float32)
    lanes = lanes_of(2 * span)
    table = jnp.pad(table, ((0, 0), (0, lanes - 3 * span)))
    taps = jnp.pad(
        encoder_filter.astype(jnp.float32),
        ((0, 0), (0, basis_count), (0, lanes_of(cols_in) - tap_count)),
    ).reshape(rows_in * 2 * basis_count, -1)
    own_width = channels // lax.axis_size("ch")
    sizes = (lax.axis_size("lat"), lax.axis_size("lon"))
    plan = (rows_dev, cols_dev, basis_count, layers)
    outs = run_net(
        plan,
        sizes,
        input_field.reshape(rows_in * cols_in, in_width),
        taps,
        row_owner,
        encoder_weight,
        table,
        block_weights,
        cotangent.reshape(cell_count, channels),
    )
    current, gradient = (field.reshape(rows_dev, cols_dev, channels) for field in outs[:2])
    sums = [value.astype(jnp.float32) for value in outs[2:]]
    block_sum, encoder_sum = jnp.stack(sums[:-1]), sums[-1]
    cells_total = cell_count * lax.axis_size("lon") * lax.axis_size(("lat", "ch"))
    normalizer = 1.0 / math.sqrt(cells_total)
    block_grads = (block_sum * normalizer).reshape(layers, basis_count * channels, own_width)
    encoder_grad = encoder_sum * normalizer
    return (current, gradient, block_grads, encoder_grad)


def solution(mesh):
    placed = (
        P(("ens", "lat", "ch"), "lon", None),
        P(("lat", "ch"), None, None),
        P(("ens", "lat", "ch")),
        P(),
        P(("lat", "ch"), None, None, None),
        P(("lat", "ch")),
        P(),
        P(("ens", "lat", "ch"), "lon", None),
    )
    return jax.shard_map(
        per_device,
        mesh=mesh,
        in_specs=placed,
        out_specs=(
            P(("ens", "lat", "ch"), "lon", None),
            P(("ens", "lat", "ch"), "lon", None),
            P("ens", None, "ch"),
            P("ens", "ch"),
        ),
        check_vma=False,
    )
```

```python
import functools
import math

import jax
import jax.numpy as jnp
from jax import lax
from jax.experimental import pallas as pl
from jax.experimental.pallas import tpu as pltpu
from jax.sharding import PartitionSpec as P

REACH = 8
TAP_REACH = 2
TILE = 16
MESH = pl.DeviceIdType.MESH
BF16 = jnp.bfloat16
F32 = jnp.float32


def along(axis, steps):
    count = lax.axis_size(axis)
    return {axis: lax.rem(lax.axis_index(axis) + steps + count, count)}


def neighbour(row_step, col_step):
    ch_count = lax.axis_size("ch")
    bands = lax.axis_size("lat") * ch_count
    band = lax.axis_index("lat") * ch_count + lax.axis_index("ch")
    band = lax.rem(band + row_step + bands, bands)
    target = {}
    if row_step:
        target = {"lat": band // ch_count, "ch": lax.rem(band, ch_count)}
    if col_step:
        target.update(along("lon", col_step))
    return target


AROUND = [(r, c) for r in (-1, 0, 1) for c in (-1, 0, 1) if r or c]


def greet():
    targets = [neighbour(r, c) for r, c in AROUND]
    for axis in ("ch", "lat", "lon"):
        targets += [along(axis, step) for step in range(1, lax.axis_size(axis))]
    barrier = pltpu.get_barrier_semaphore()
    for target in targets:
        pl.semaphore_signal(barrier, inc=1, device_id=target, device_id_type=MESH)
    pl.semaphore_wait(barrier, len(targets))


class Sender:
    def __init__(self, sems):
        self.ssem, self.rsem = sems
        self.pending = []

    def send(self, source, target, slot, device):
        copy = pltpu.make_async_remote_copy(
            src_ref=source,
            dst_ref=target,
            send_sem=self.ssem.at[slot],
            recv_sem=self.rsem.at[slot],
            device_id=device,
            device_id_type=MESH,
        )
        copy.start()
        self.pending.append(copy)

    def settle(self):
        for copy in self.pending:
            copy.wait()
        self.pending = []


class GradSum(Sender):
    def __init__(self, result, bufs):
        super().__init__(bufs[-2:])
        self.result = result
        self.source, self.rec_ch, self.part, self.rec_lat, self.strip, self.rec_pair, self.half, self.rec_far, self.piece = bufs[:-2]
        self.width = self.part.shape[1]
        self.lat, self.lon = lax.axis_size("lat"), lax.axis_size("lon")
        self.height = self.strip.shape[0]
        self.span = self.piece.shape[0]
        self.pair = self.height // self.span
        self.far = self.lon // self.pair
        self.side = lax.rem(lax.axis_index("lon"), self.pair)

    @staticmethod
    def scratch(sizes, rows, columns):
        lat, lon = sizes
        width = columns // 2
        height = rows // lat
        pair = 2 if lon % 2 == 0 and height % (2 * TILE) == 0 else 1
        span, far = height // pair, lon // pair
        count = 1 + 2 * (lat - 1) + 2 * (pair - 1) + far - 1
        return [
            pltpu.VMEM((rows, columns), BF16),
            pltpu.VMEM((rows, width), BF16),
            pltpu.VMEM((rows, width), BF16),
            pltpu.VMEM((lat - 1, height, width), BF16),
            pltpu.VMEM((height, width), BF16),
            pltpu.VMEM((span, width), BF16),
            pltpu.VMEM((span, width), BF16),
            pltpu.VMEM((far - 1, span, width), BF16),
            pltpu.VMEM((span, width), BF16),
            pltpu.SemaphoreType.DMA((count,)),
            pltpu.SemaphoreType.DMA((count,)),
        ]

    def columns(self, half):
        return pl.ds(pl.multiple_of(half * self.width, self.width), self.width)

    @staticmethod
    def stretch(owner, size):
        return pl.ds(pl.multiple_of(owner * size, size), size)

    def start_ch(self):
        other = 1 - lax.axis_index("ch")
        self.send(self.source.at[:, self.columns(other)], self.rec_ch, 0, {"ch": other})

    def start_lat(self):
        self.settle()
        own = self.source[:, self.columns(lax.axis_index("ch"))].astype(F32)
        self.part[...] = (own + self.rec_ch[...].astype(F32)).astype(BF16)
        for step in range(1, self.lat):
            peer = along("lat", step)
            rows = self.stretch(peer["lat"], self.height)
            self.send(self.part.at[rows], self.rec_lat.at[step - 1], step, peer)

    def start_lon(self):
        self.settle()
        total = self.part[self.stretch(lax.axis_index("lat"), self.height), :].astype(F32)
        for step in range(1, self.lat):
            total = total + self.rec_lat[step - 1].astype(F32)
        self.strip[...] = total.astype(BF16)
        if self.pair > 1:
            rows = self.stretch(1 - self.side, self.span)
            self.send(self.strip.at[rows], self.rec_pair, self.lat, along("lon", 1 - 2 * self.side))

    def start_far(self):
        self.settle()
        total = self.strip[self.stretch(self.side, self.span), :].astype(F32)
        if self.pair > 1:
            total = total + self.rec_pair[...].astype(F32)
        self.half[...] = total.astype(BF16)
        for step in range(1, self.far):
            self.send(
                self.half, self.rec_far.at[step - 1], self.lat + step, along("lon", self.pair * step)
            )

    def gather_lon(self):
        self.settle()
        total = self.half[...].astype(F32)
        for step in range(1, self.far):
            total = total + self.rec_far[step - 1].astype(F32)
        self.piece[...] = total.astype(BF16)
        offset = lax.axis_index("lat") * self.height + self.side * self.span
        rows = pl.ds(pl.multiple_of(offset, TILE), self.span)
        self.result[rows, :] = self.piece[...]
        if self.pair > 1:
            slot = self.lat + self.far
            self.send(self.piece, self.result.at[rows], slot, along("lon", 1 - 2 * self.side))

    def gather_lat(self):
        self.settle()
        rows = self.stretch(lax.axis_index("lat"), self.height)
        for step in range(1, self.lat):
            slot = self.lat + self.far + self.pair - 2 + step
            self.send(self.result.at[rows], self.result.at[rows], slot, along("lat", step))

    def finish(self):
        self.settle()


STAGES = ("start_ch", "start_lat", "start_lon", "start_far", "gather_lon", "gather_lat", "finish")


class Halo(Sender):
    def __init__(self, bufs):
        super().__init__(bufs[-2:])
        self.out_side, self.out_row, self.in_side, self.in_row = bufs[:-2]

    @staticmethod
    def scratch(rows, cols, width, row_blocks):
        return [
            pltpu.VMEM((2, rows * REACH, width), BF16),
            pltpu.VMEM((row_blocks, cols, width), BF16),
            pltpu.VMEM((2, rows * REACH, width), BF16),
            pltpu.VMEM((6, cols, width), BF16),
            pltpu.SemaphoreType.DMA((8,)),
            pltpu.SemaphoreType.DMA((8,)),
        ]

    def start(self, row_block_of):
        self.send(self.out_side.at[0], self.in_side.at[1], 0, neighbour(0, -1))
        self.send(self.out_side.at[1], self.in_side.at[0], 1, neighbour(0, 1))
        slot = 2
        for row_step in (-1, 1):
            for col_step in (-1, 0, 1):
                place = (0 if row_step == 1 else 3) + 1 - col_step
                self.send(
                    self.out_row.at[row_block_of(row_step, col_step)],
                    self.in_row.at[place],
                    slot,
                    neighbour(row_step, col_step),
                )
                slot += 1


def edge_flags():
    ch_count = lax.axis_size("ch")
    bands = lax.axis_size("lat") * ch_count
    band = lax.axis_index("lat") * ch_count + lax.axis_index("ch")
    return band > 0, band < bands - 1


def extend(halo, state, ext, rows, cols):
    span = cols + 2 * REACH
    west, east = halo.in_side[0].astype(F32), halo.in_side[1].astype(F32)
    for row in range(rows):
        low, high = row * REACH, (row + 1) * REACH
        line = jnp.concatenate(
            [west[low:high], state[row * cols : (row + 1) * cols], east[low:high]], axis=0
        )
        ext[(row + 1) * span : (row + 2) * span, :] = line.astype(BF16)
    for first, row, flag in zip((0, 3), (0, rows + 1), edge_flags()):
        line = jnp.concatenate(
            [
                halo.in_row[first].astype(F32)[cols - REACH :],
                halo.in_row[first + 1].astype(F32),
                halo.in_row[first + 2].astype(F32)[:REACH],
            ],
            axis=0,
        )
        ext[row * span : (row + 1) * span, :] = jnp.where(flag, line, 0.0).astype(BF16)


def send_state(halo, state, rows, cols):
    pieces = [
        [state[r * cols : r * cols + REACH] for r in range(rows)],
        [state[(r + 1) * cols - REACH : (r + 1) * cols] for r in range(rows)],
    ]
    for side in range(2):
        halo.out_side[side] = jnp.concatenate(pieces[side], axis=0).astype(BF16)
    halo.out_row[0] = state[:cols].astype(BF16)
    halo.out_row[1] = state[(rows - 1) * cols :].astype(BF16)
    halo.start(lambda row_step, col_step: 0 if row_step == -1 else 1)


def send_spread(halo, spread, rows, cols):
    span = cols + 2 * REACH
    west = [spread[(r + 1) * span : (r + 1) * span + REACH, :] for r in range(rows)]
    east = [spread[(r + 2) * span - REACH : (r + 2) * span, :] for r in range(rows)]
    halo.out_side[0] = jnp.concatenate(west, axis=0).astype(BF16)
    halo.out_side[1] = jnp.concatenate(east, axis=0).astype(BF16)
    for block, row in enumerate((0, rows + 1)):
        base = row * span
        halo.out_row[2 * block] = spread[base + REACH : base + REACH + cols, :].astype(BF16)
        corners = [spread[base : base + REACH, :], spread[base + span - REACH : base + span, :]]
        if cols > 2 * REACH:
            corners.insert(1, jnp.zeros((cols - 2 * REACH, spread.shape[1]), F32))
        halo.out_row[2 * block + 1] = jnp.concatenate(corners, axis=0).astype(BF16)
    halo.start(
        lambda row_step, col_step: (0 if row_step == -1 else 2) + (1 if col_step else 0)
    )


def take_spread(halo, spread, gradient, rows, cols):
    span = cols + 2 * REACH
    west, east = halo.in_side[0].astype(F32), halo.in_side[1].astype(F32)
    outer = {}
    for first, row, flag in zip((0, 3), (0, rows - 1), edge_flags()):
        line = halo.in_row[first + 1].astype(F32)
        rim_west = halo.in_row[first].astype(F32)[cols - REACH :]
        rim_east = halo.in_row[first + 2].astype(F32)[:REACH]
        rims = [rim_west, rim_east]
        if cols > 2 * REACH:
            rims.insert(1, jnp.zeros((cols - 2 * REACH, line.shape[1]), F32))
        outer[row] = jnp.where(flag, line + jnp.concatenate(rims, axis=0), 0.0)
    result = []
    for row in range(rows):
        low, high = row * REACH, (row + 1) * REACH
        rims = [west[low:high], east[low:high]]
        if cols > 2 * REACH:
            rims.insert(1, jnp.zeros((cols - 2 * REACH, west.shape[1]), F32))
        base = (row + 1) * span + REACH
        line = spread[base : base + cols, :] + jnp.concatenate(rims, axis=0)
        if row in outer:
            line = line + outer[row]
        result.append(gradient[row * cols : (row + 1) * cols].astype(F32) + line)
    return result


def aligned(index, size):
    return pl.ds(pl.multiple_of(index * size, size), size)


GROUP = 16


def over_rows(rows, body):
    group = GROUP if rows % GROUP == 0 else 1

    def step(index, carry):
        for inner in range(group):
            body(index * group + inner)
        return carry

    lax.fori_loop(0, rows // group, step, 0)


def make_bands(base, bands, rows, cols, basis_count):
    width = base.shape[1]

    def one(row):
        table = base[aligned(row, 2 * basis_count), :]
        for k in range(basis_count):
            line = jnp.broadcast_to(table[k : k + 1], (cols, width))
            moved = pltpu.roll(line, 0, 1, stride=1, stride_axis=0)
            start = pl.multiple_of((row * basis_count + k) * cols, cols)
            bands[pl.ds(start, cols), :] = moved.astype(BF16)

    over_rows(rows, one)


def stencil(bands, ext, features, rows, cols, basis_count):
    span = cols + 2 * REACH
    channels = ext.shape[1]

    def one(row):
        lhs = bands[aligned(row, basis_count * cols), :][:, : 3 * span]
        rhs = ext[pl.ds(pl.multiple_of(row * span, span), 3 * span), :]
        out = jnp.dot(lhs, rhs, preferred_element_type=F32).astype(BF16)
        for k in range(basis_count):
            features[aligned(row, cols), k * channels : (k + 1) * channels] = out[
                k * cols : (k + 1) * cols
            ]

    over_rows(rows, one)


def adjoint(bands, errs, spread, rows, cols, basis_count):
    span = cols + 2 * REACH
    spread[...] = jnp.zeros_like(spread)

    def one(row):
        lhs = bands[aligned(row, basis_count * cols), :][:, : 3 * span]
        rhs = errs[aligned(row, basis_count * cols), :]
        out = lax.dot_general(lhs, rhs, (((0,), (0,)), ((), ())), preferred_element_type=F32)
        place = pl.ds(pl.multiple_of(row * span, span), 3 * span)
        spread[place, :] = spread[place, :] + out

    over_rows(rows, one)


def rows_product(left, right):
    return lax.dot_general(left, right, (((0,), (0,)), ((), ())), preferred_element_type=F32)
TAPS_LEFT = TAP_REACH


class InputHalo(Sender):
    def __init__(self, bufs):
        super().__init__(bufs[-2:])
        (
            self.edges,
            self.out_cols,
            self.out_table,
            self.in_cols,
            self.in_row,
            self.in_table,
            self.in_tile,
        ) = bufs[:-2]

    @staticmethod
    def scratch(rows_in, cols_in, width, table_rows, lanes):
        return [
            pltpu.VMEM((3, rows_in, width), F32),
            pltpu.VMEM((3, rows_in, width), BF16),
            pltpu.VMEM((2, table_rows, lanes), F32),
            pltpu.VMEM((3, rows_in, width), BF16),
            pltpu.VMEM((2, cols_in, width), BF16),
            pltpu.VMEM((2, table_rows, lanes), F32),
            pltpu.VMEM((4, TILE, width), BF16),
            pltpu.SemaphoreType.DMA((10,)),
            pltpu.SemaphoreType.DMA((10,)),
        ]

    def start(self, field, table, owner, rows_in, cols_in):
        first = own_first_row(rows_in // 2)
        table_rows = self.out_table.shape[1]
        for block, row, target in ((0, 0, first - 1), (1, rows_in - 1, first + rows_in // 2)):
            feeds = jnp.where(owner[row] == target, 1.0, 0.0)
            self.out_table[block] = table[row * table_rows : (row + 1) * table_rows, :] * feeds
        last = (rows_in - 1) * cols_in
        lines = (field.at[pl.ds(0, cols_in)], field.at[pl.ds(last, cols_in)])
        slot = 0
        for block, row_step in ((0, -1), (1, 1)):
            self.send(lines[block], self.in_row.at[1 - block], slot, neighbour(row_step, 0))
            base = block * last
            west = field.at[pl.ds(base, TILE)]
            east = field.at[pl.ds(base + cols_in - TILE, TILE)]
            place = 2 * (1 - block)
            self.send(west, self.in_tile.at[place + 1], slot + 1, neighbour(row_step, -1))
            self.send(east, self.in_tile.at[place], slot + 2, neighbour(row_step, 1))
            slot += 3

        def one(row):
            low = field[pl.ds(pl.multiple_of(row * cols_in, TILE), TILE), :].astype(F32)
            start = pl.multiple_of(row * cols_in + cols_in - TILE, TILE)
            high = field[pl.ds(start, TILE), :].astype(F32)
            self.edges[0, pl.ds(row, 1), :] = high[TILE - 2 : TILE - 1]
            self.edges[1, pl.ds(row, 1), :] = high[TILE - 1 : TILE]
            self.edges[2, pl.ds(row, 1), :] = low[0:1]

        over_rows(rows_in, one)
        self.out_cols[...] = self.edges[...].astype(BF16)
        self.send(self.out_cols.at[pl.ds(0, 2)], self.in_cols.at[pl.ds(0, 2)], 6, neighbour(0, 1))
        self.send(self.out_cols.at[2], self.in_cols.at[2], 7, neighbour(0, -1))
        self.send(self.out_table.at[0], self.in_table.at[1], 8, neighbour(-1, 0))
        self.send(self.out_table.at[1], self.in_table.at[0], 9, neighbour(1, 0))


def own_first_row(rows):
    return (lax.axis_index("lat") * lax.axis_size("ch") + lax.axis_index("ch")) * rows


def tap_matrix(table, basis_count, cols, cols_in):
    lanes = table.shape[1]
    blocks = []
    for k in range(basis_count):
        line = jnp.broadcast_to(table[k : k + 1], (cols, lanes))
        moved = pltpu.roll(line, 0, 1, stride=2, stride_axis=0)
        wrapped = pltpu.roll(moved, cols_in + TILE - TAPS_LEFT, 1)
        moved = pltpu.roll(moved, lanes - TAPS_LEFT, 1)
        lane = lax.broadcasted_iota(jnp.int32, (cols, lanes), 1)
        at_end = (lane >= cols_in + TILE - TAPS_LEFT) & (lane < cols_in + TILE)
        blocks.append(jnp.where(at_end, wrapped, moved))
    return jnp.concatenate(blocks, axis=0)[:, : cols_in + TILE].astype(BF16)


def filtered_row(table, line, left_two, left_one, right, basis_count, cols, cols_in):
    width = line.shape[1]
    place = lax.broadcasted_iota(jnp.int32, (TILE, width), 0)
    tile = jnp.where(place == 0, jnp.broadcast_to(right, (TILE, width)), 0.0)
    tile = jnp.where(place == TILE - 2, jnp.broadcast_to(left_two, (TILE, width)), tile)
    tile = jnp.where(place == TILE - 1, jnp.broadcast_to(left_one, (TILE, width)), tile)
    rhs = jnp.concatenate([line, tile.astype(BF16)], axis=0)
    lhs = tap_matrix(table, basis_count, cols, cols_in)
    return jnp.dot(lhs, rhs, preferred_element_type=F32).astype(BF16)


def finish_encode(halo, field, table, owner, filtered, latent_in, plan, rows_in, cols_in):
    rows, cols, basis_count, _ = plan
    table_rows = halo.out_table.shape[1]
    block = basis_count * cols
    width = field.shape[1]
    halo.settle()
    halo.edges[...] = halo.in_cols[...].astype(F32)

    def one(row):
        sides = [halo.edges[index, pl.ds(row, 1), :] for index in range(3)]
        line = field[aligned(row, cols_in), :]
        taps = table[aligned(row, table_rows), :]
        filtered[aligned(row + 1, block), :] = filtered_row(
            taps, line, *sides, basis_count, cols, cols_in
        )

    over_rows(rows_in, one)
    for side, row in ((0, 0), (1, rows_in + 1)):
        west = halo.in_tile[2 * side].astype(F32)
        east = halo.in_tile[2 * side + 1].astype(F32)
        filtered[row * block : (row + 1) * block, :] = filtered_row(
            halo.in_table[side],
            halo.in_row[side],
            west[TILE - 2 : TILE - 1],
            west[TILE - 1 : TILE],
            east[0:1],
            basis_count,
            cols,
            cols_in,
        )
    first = own_first_row(rows)
    for row in range(rows):
        total = None
        for offset in range(-1, 3):
            source = 2 * row + offset
            term = filtered[(source + 1) * block : (source + 2) * block, :].astype(F32)
            if 0 <= source < rows_in:
                term = term * jnp.where(owner[source] == first + row, 1.0, 0.0)
            total = term if total is None else total + term
        total = total.astype(BF16)
        for k in range(basis_count):
            latent_in[row * cols : (row + 1) * cols, k * width : (k + 1) * width] = total[
                k * cols : (k + 1) * cols
            ]


def lanes_of(count):
    return -(-(count + 2 * TILE) // 128) * 128


def net_kernel(plan, *refs):
    rows, cols, basis_count, layers = plan
    field, table, owner, encoder_weight, base, weights, cotangent = refs[:7]
    state_out, latent_grad = refs[7:9]
    results = refs[9 : 10 + layers]
    rest = list(refs[10 + layers :])
    bands, ext, spread, errs, features, preact, filtered, latent_in = rest[:8]
    input_halo = InputHalo(rest[8:17])
    rest = rest[17:]
    halos = []
    for _ in range(2 * layers):
        halos.append(Halo(rest[:6]))
        rest = rest[6:]
    sums = []
    for index in range(layers + 1):
        sums.append(GradSum(results[index], rest[:11]))
        rest = rest[11:]
    channels = ext.shape[1]
    progress = [0] * (layers + 1)

    def advance(index):
        getattr(sums[index], STAGES[progress[index]])()
        progress[index] += 1

    greet()
    rows_in = owner.shape[0]
    cols_in = field.shape[0] // rows_in
    input_halo.start(field, table, owner, rows_in, cols_in)
    make_bands(base, bands, rows, cols, basis_count)
    finish_encode(input_halo, field, table, owner, filtered, latent_in, plan, rows_in, cols_in)
    state = jnp.dot(latent_in[...], encoder_weight[...], preferred_element_type=F32)
    state = state.astype(BF16).astype(F32)
    for layer in range(layers):
        send_state(halos[layer], state, rows, cols)
        halos[layer].settle()
        extend(halos[layer], state, ext, rows, cols)
        stencil(bands, ext, features.at[layer], rows, cols, basis_count)
        pre = jnp.dot(features[layer], weights[layer], preferred_element_type=F32)
        preact[layer] = pre
        state = (state + pre / (1.0 + jnp.exp(-pre))).astype(BF16).astype(F32)
    state_out[...] = state.astype(BF16)

    gradient = cotangent[...].astype(F32)
    for layer in reversed(range(layers)):
        pre = preact[layer]
        sigma = 1.0 / (1.0 + jnp.exp(-pre))
        act_grad = (gradient * sigma * (1.0 + pre * (1.0 - sigma))).astype(BF16)
        for k in range(basis_count):
            block = weights[layer, k * channels : (k + 1) * channels, :]
            out = lax.dot_general(
                act_grad, block, (((1,), (1,)), ((), ())), preferred_element_type=F32
            ).astype(BF16)
            for row in range(rows):
                start = (row * basis_count + k) * cols
                errs[start : start + cols, :] = out[row * cols : (row + 1) * cols]
        adjoint(bands, errs, spread, rows, cols, basis_count)
        halo = halos[layers + layer]
        send_spread(halo, spread, rows, cols)
        sums[layer].source[...] = rows_product(features[layer], act_grad).astype(BF16)
        for other in range(layers - 1, layer - 1, -1):
            advance(other)
        halo.settle()
        for other in range(layers - 1, layer - 1, -1):
            advance(other)
        lines = take_spread(halo, spread, gradient, rows, cols)
        gradient = jnp.concatenate(lines, axis=0).astype(BF16).astype(F32)
    latent_grad[...] = gradient.astype(BF16)
    sums[layers].source[...] = rows_product(latent_in[...], gradient.astype(BF16)).astype(BF16)
    advance(layers)
    while min(progress) < len(STAGES):
        for index in [layers] + list(range(layers))[::-1]:
            if progress[index] < len(STAGES):
                advance(index)


def run_net(plan, sizes, field_in, table, owner, encoder_weight, base, weights, cotangent):
    rows, cols, basis_count, layers = plan
    cells, channels = rows * cols, weights.shape[2]
    features = basis_count * channels
    span = cols + 2 * REACH
    rows_in = owner.shape[0]
    in_features = encoder_weight.shape[0]
    heights = [features] * layers + [in_features]
    scratch = [
        pltpu.VMEM((rows * basis_count * cols, base.shape[1]), BF16),
        pltpu.VMEM(((rows + 2) * span, channels), BF16),
        pltpu.VMEM(((rows + 2) * span, channels), F32),
        pltpu.VMEM((rows * basis_count * cols, channels), BF16),
        pltpu.VMEM((layers, cells, features), BF16),
        pltpu.VMEM((layers, cells, channels), F32),
        pltpu.VMEM(((rows_in + 2) * basis_count * cols, field_in.shape[1]), BF16),
        pltpu.VMEM((cells, in_features), BF16),
    ]
    scratch += InputHalo.scratch(
        rows_in, field_in.shape[0] // rows_in, field_in.shape[1], table.shape[0] // rows_in, table.shape[1]
    )
    for index in range(2 * layers):
        scratch += Halo.scratch(rows, cols, channels, 2 if index < layers else 4)
    for height in heights:
        scratch += GradSum.scratch(sizes, height, channels)
    vmem = pl.BlockSpec(memory_space=pltpu.VMEM)
    field = jax.ShapeDtypeStruct((cells, channels), BF16)
    grads = [jax.ShapeDtypeStruct((height, channels // 2), BF16) for height in heights]
    return pl.pallas_call(
        functools.partial(net_kernel, plan),
        out_shape=[field, field] + grads,
        in_specs=[vmem, vmem, pl.BlockSpec(memory_space=pltpu.SMEM)] + [vmem] * 4,
        out_specs=[vmem] * (3 + layers),
        scratch_shapes=scratch,
        compiler_params=pltpu.CompilerParams(
            collective_id=0, has_side_effects=True, vmem_limit_bytes=56 << 20
        ),
    )(field_in, table, owner, encoder_weight, base, weights, cotangent)


def per_device(
    input_field,
    encoder_filter,
    row_owner,
    encoder_weight,
    disco_basis,
    row_widths,
    block_weights,
    cotangent,
):
    rows_in, cols_in, in_width = input_field.shape
    rows_dev = rows_in // 2
    cols_dev = cols_in // 2
    basis_count = encoder_filter.shape[1]
    tap_count = encoder_filter.shape[2]
    channels = block_weights.shape[2]
    layers = block_weights.shape[0]
    cell_count = rows_dev * cols_dev
    offsets = jnp.abs(jnp.arange(2 * REACH + 1, dtype=jnp.int32) - REACH)
    keep = offsets[None, :] <= row_widths[:, None]
    masked = jnp.where(keep[:, None, None, :], disco_basis, jnp.zeros_like(disco_basis))
    span = cols_dev + 2 * REACH
    table = jnp.pad(masked, ((0, 0), (0, basis_count), (0, 0), (0, span - masked.shape[3])))
    table = table.reshape(rows_dev * 2 * basis_count, 3 * span).astype(jnp.float32)
    lanes = lanes_of(2 * span)
    table = jnp.pad(table, ((0, 0), (0, lanes - 3 * span)))
    taps = jnp.pad(
        encoder_filter.astype(jnp.float32),
        ((0, 0), (0, basis_count), (0, lanes_of(cols_in) - tap_count)),
    ).reshape(rows_in * 2 * basis_count, -1)
    own_width = channels // lax.axis_size("ch")
    sizes = (lax.axis_size("lat"), lax.axis_size("lon"))
    plan = (rows_dev, cols_dev, basis_count, layers)
    outs = run_net(
        plan,
        sizes,
        input_field.reshape(rows_in * cols_in, in_width),
        taps,
        row_owner,
        encoder_weight,
        table,
        block_weights,
        cotangent.reshape(cell_count, channels),
    )
    current, gradient = (field.reshape(rows_dev, cols_dev, channels) for field in outs[:2])
    sums = [value.astype(jnp.float32) for value in outs[2:]]
    block_sum, encoder_sum = jnp.stack(sums[:-1]), sums[-1]
    cells_total = cell_count * lax.axis_size("lon") * lax.axis_size(("lat", "ch"))
    normalizer = 1.0 / math.sqrt(cells_total)
    block_grads = (block_sum * normalizer).reshape(layers, basis_count * channels, own_width)
    encoder_grad = encoder_sum * normalizer
    return (current, gradient, block_grads, encoder_grad)


def solution(mesh):
    placed = (
        P(("ens", "lat", "ch"), "lon", None),
        P(("lat", "ch"), None, None),
        P(("ens", "lat", "ch")),
        P(),
        P(("lat", "ch"), None, None, None),
        P(("lat", "ch")),
        P(),
        P(("ens", "lat", "ch"), "lon", None),
    )
    return jax.shard_map(
        per_device,
        mesh=mesh,
        in_specs=placed,
        out_specs=(
            P(("ens", "lat", "ch"), "lon", None),
            P(("ens", "lat", "ch"), "lon", None),
            P("ens", None, "ch"),
            P("ens", "ch"),
        ),
        check_vma=False,
    )
```
